128 devices in a mesh: tgt: 16 (over z, x), src: 8 (over y, core).
Axes of the slice: x: 4, y: 4, z: 4, core: 2. Of those that a mesh axis runs over, the one named last changes fastest.
Arguments:
- points: bfloat16 [262144, 256], P(('tgt', 'src')), may hold values from -0.4 to 0.4
- weights: bfloat16 [262144, 64], P(('tgt', 'src')), may hold values from -6 to 6
- near_list: int32 [2048, 16], P(('tgt', 'src')), may hold values from -1 to 127, as said below
- far_list: int32 [2048, 3, 8], P('tgt', None, 'src'), may hold values from -1 to 63, as said below
- skel_index: int32 [896, 256], P(('tgt', 'src')), may hold values from 0 to 2047, as said below
- equiv_weights: bfloat16 [896, 256, 64], P(('tgt', 'src')), may hold values from -6 to 6
Outputs:
- potential: float32 [262144, 64], P(('tgt', 'src'))
The draws below stay inside these ranges and needn't reach their ends.
Inputs may be any that keep to these rules, and one draw needn't show every extreme that they name: `near_list`: row b lists blocks of b's group of 128 blocks by their index within the group: first b itself, then distinct other blocks; after a row's live entries all are -1; every row has 4 or more live entries. `far_list`: entry [b, l, c] is -1 or a level-l node owned by a device of src index c, numbered as the owner's tgt index times (16 // (4 * 2 ** l)) plus the node's number among the owner's level-l nodes. `skel_index`: Level-l nodes of a device cover 4 * 128 * 2 ** l consecutive points of that device each, in order; a node's 256 entries are increasing indices of the device's points inside the node.
All inputs are finite; a program needn't handle non-finite values.
Results may differ from the reference program's by a relative error of at most 0.0023.
Values may be sent and summed in bfloat16 or wider, within the bound.
No kernel may reach another device: no remote copies, remote signals or barrier semaphores. Data moves between devices by JAX's collectives and lax.ppermute only.
A program may use at most 192 MiB of HBM per device.

```python
import jax
import jax.numpy as jnp
from jax import lax

E = 256
WCOL = 64
BLK = 128
RANK = 256
NEAR = 16
LEVELS = 3
BLK_DEV = 16
NODE_DEV = 7
NPTS = 262144
NODES = 896
N_TGT = 16
N_SRC = 8
DEVICES = 128


def random_signs(key, shape):
    return 2.0 * jax.random.randint(key, shape, 0, 2).astype(jnp.float32) - 1.0


def draw_points(key, part):
    centre_size = 0.09
    scale_low = 0.85
    scale_high = 1.15
    noise = jnp.clip(0.0625 * jax.random.normal(jax.random.fold_in(key, 44), (DEVICES, BLK_DEV, BLK, E), jnp.float32), -0.25, 0.25)
    centre = centre_size * random_signs(jax.random.fold_in(key, 41), (E,))
    device_part = 0.02 * random_signs(jax.random.fold_in(key, 42), (DEVICES, E))
    block_scale = jax.random.uniform(jax.random.fold_in(key, 43), (DEVICES, BLK_DEV, 1, 1), jnp.float32, scale_low, scale_high)
    base = (centre[None, :] + device_part)[:, None, None, :]
    values = block_scale * base + noise
    return values.reshape(DEVICES * BLK_DEV * BLK, E).astype(jnp.bfloat16)


def draw_near_list(key, part):
    group_blocks = N_SRC * BLK_DEV
    row_count = BLK_DEV * DEVICES
    row_ids = jnp.arange(row_count, dtype=jnp.int32)
    own_block = row_ids % group_blocks
    row_keys = jax.random.split(jax.random.fold_in(key, 11), row_count)

    def pick_neighbours(row_key):
        return jax.random.permutation(row_key, group_blocks - 1)[:NEAR - 1]
    neighbours = jax.vmap(pick_neighbours)(row_keys).astype(jnp.int32)
    neighbours = (own_block[:, None] + 1 + neighbours) % group_blocks
    entries = jnp.concatenate([own_block[:, None], neighbours], axis=1)
    device_shift = jax.random.randint(jax.random.fold_in(key, 12), (DEVICES,), 0, 3)
    device_cap = jnp.right_shift(jnp.int32(NEAR), device_shift)[row_ids // BLK_DEV]
    live_count = jax.random.randint(jax.random.fold_in(key, 13), (row_count,), NEAR // 4, NEAR + 1)
    live_count = jnp.minimum(live_count, jnp.maximum(device_cap, NEAR // 4))
    live_count = live_count.at[0].set(NEAR).at[1].set(NEAR // 4)
    slot_index = jnp.arange(NEAR, dtype=jnp.int32)[None, :]
    return jnp.where(slot_index < live_count[:, None], entries, -1).astype(jnp.int32)


def draw_far_list(key, part):
    row_count = BLK_DEV * DEVICES
    level_sizes = jnp.array([N_TGT * (BLK_DEV // (4 * 2 ** tree_level)) for tree_level in range(LEVELS)], jnp.int32)
    raw_draw = jax.random.randint(jax.random.fold_in(key, 21), (row_count, LEVELS, N_SRC), 0, 16777216)
    values = raw_draw % level_sizes[None, :, None]
    is_live = jax.random.randint(jax.random.fold_in(key, 22), (row_count, LEVELS, N_SRC), 0, 4) < 3
    values = values.at[0, 0, :].set(level_sizes[0] - 1)
    is_live = is_live.at[0].set(True).at[1].set(False)
    return jnp.where(is_live, values, -1).astype(jnp.int32)


def draw_skel_index(key, part):
    row_count = NODE_DEV * DEVICES
    local_node = jnp.arange(row_count, dtype=jnp.int32) % NODE_DEV
    first_count = BLK_DEV // 4
    second_count = BLK_DEV // 8
    tree_level = (local_node >= first_count).astype(jnp.int32) + (local_node >= first_count + second_count).astype(jnp.int32)
    within = local_node - jnp.where(tree_level == 0, 0, jnp.where(tree_level == 1, first_count, first_count + second_count))
    node_size = jnp.left_shift(jnp.int32(4 * BLK), tree_level)
    stride_size = node_size // RANK
    jitter = jax.random.randint(jax.random.fold_in(key, 31), (row_count, RANK), 0, 16777216) % stride_size[:, None]
    jitter = jitter.at[:, 0].set(0)
    jitter = jitter.at[:, RANK - 1].set(stride_size - 1)
    offset = jnp.arange(RANK, dtype=jnp.int32)[None, :] * stride_size[:, None] + jitter
    return ((within * node_size)[:, None] + offset).astype(jnp.int32)


def shard_levels(own_key, shape, pieces, least, top_value):
    def one(dim, parts):
        heights = jax.random.uniform(jax.random.fold_in(jax.random.fold_in(own_key, 6), dim), (parts,), jnp.float32, least / len(pieces), top_value / len(pieces))
        return jnp.repeat(jnp.exp(heights), shape[dim] // parts).reshape((-1,) + (1,) * (len(shape) - dim - 1))

    factor_of = one(*pieces[0])
    for cut in pieces[1:]:
        factor_of = factor_of * one(*cut)
    return factor_of


def bell_draw(own_key, shape, deviation, reach, cuts=(), held_as=jnp.bfloat16):
    gain = shard_levels(own_key, shape, cuts, -0.22, 0.18) if cuts else 1.0
    values = jax.random.normal(own_key, shape, jnp.float32) * deviation * gain
    return jnp.minimum(jnp.maximum(values, -reach), reach).astype(held_as)


def setup_inputs(seed: int = 0) -> dict:
    arg_keys = jax.random.split(jax.random.key(seed), 7)
    points = draw_points(jax.random.fold_in(arg_keys[6], 71), 0)
    weights = bell_draw(arg_keys[1], (NPTS, WCOL), 1.0, 6.0, ((0, 128),))
    near_list = draw_near_list(jax.random.fold_in(arg_keys[6], 71), 0)
    far_list = draw_far_list(jax.random.fold_in(arg_keys[6], 71), 0)
    skel_index = draw_skel_index(jax.random.fold_in(arg_keys[6], 71), 0)
    equiv_weights = bell_draw(arg_keys[5], (NODES, RANK, WCOL), 1.0, 6.0, ((0, 128),))
    return {"points": points, "weights": weights, "near_list": near_list, "far_list": far_list, "skel_index": skel_index, "equiv_weights": equiv_weights}


kernel_rate = 2.0


def tile_kernel(targets, target_norms, sources, source_norms, live_mask):
    dot_terms = jnp.einsum("bie,bse->bis", targets.astype(jnp.float32), sources.astype(jnp.float32))
    sq_dist = target_norms[:, :, None] + source_norms[:, None, :] - 2.0 * dot_terms
    return jnp.where(live_mask[:, None, :], jnp.exp(-kernel_rate * sq_dist), 0.0).astype(jnp.bfloat16)


def apply_tile(kernel, source_weights):
    return jnp.einsum("bis,bsw->biw", kernel.astype(jnp.float32), source_weights.astype(jnp.float32))


def reference(points, weights, near_list, far_list, skel_index, equiv_weights):
    point_dev = BLK_DEV * BLK
    group_blocks = N_SRC * BLK_DEV
    group_points = N_SRC * point_dev
    node_dev = skel_index.shape[0] // (N_TGT * N_SRC)
    point_norms = jnp.sum(jnp.square(points.astype(jnp.float32)), axis=1)
    level_nodes = [BLK_DEV // (4 * 2 ** tree_level) for tree_level in range(LEVELS)]
    level_start = [sum(level_nodes[:tree_level]) for tree_level in range(LEVELS)]
    columns = jnp.arange(N_SRC, dtype=jnp.int32)

    def one_group(group_index):
        row_base = group_index * group_points
        group_pts = lax.dynamic_slice_in_dim(points, row_base, group_points, 0).reshape(group_blocks, BLK, E)
        group_norms = lax.dynamic_slice_in_dim(point_norms, row_base, group_points, 0).reshape(group_blocks, BLK)
        group_wts = lax.dynamic_slice_in_dim(weights, row_base, group_points, 0).reshape(group_blocks, BLK, WCOL)
        near_rows = lax.dynamic_slice_in_dim(near_list, group_index * group_blocks, group_blocks, 0)
        near_live = near_rows >= 0
        near_index = jnp.where(near_live, near_rows, 0)
        near_src = group_pts[near_index].reshape(group_blocks, NEAR * BLK, E)
        near_norm = group_norms[near_index].reshape(group_blocks, NEAR * BLK)
        near_wts = group_wts[near_index].reshape(group_blocks, NEAR * BLK, WCOL)
        near_mask = jnp.repeat(near_live, BLK, axis=1)
        potential = apply_tile(tile_kernel(group_pts, group_norms, near_src, near_norm, near_mask), near_wts)
        far_rows = lax.dynamic_slice_in_dim(far_list, group_index * group_blocks, group_blocks, 0)
        for tree_level in range(LEVELS):
            far_entry = far_rows[:, tree_level, :]
            far_live = far_entry >= 0
            far_entry = jnp.where(far_live, far_entry, 0)
            owner_device = (far_entry // level_nodes[tree_level]) * N_SRC + columns[None, :]
            node_rows = owner_device * node_dev + level_start[tree_level] + far_entry % level_nodes[tree_level]
            point_rows = owner_device[:, :, None] * point_dev + skel_index[node_rows]
            skel_pts = points[point_rows].reshape(group_blocks, N_SRC * RANK, E)
            skel_norms = point_norms[point_rows].reshape(group_blocks, N_SRC * RANK)
            skel_wts = equiv_weights[node_rows].reshape(group_blocks, N_SRC * RANK, WCOL)
            far_mask = jnp.repeat(far_live, RANK, axis=1)
            potential = potential + apply_tile(tile_kernel(group_pts, group_norms, skel_pts, skel_norms, far_mask), skel_wts)
        return potential.reshape(group_points, WCOL)

    result = lax.map(one_group, jnp.arange(N_TGT, dtype=jnp.int32))
    return result.reshape(N_TGT * group_points, WCOL)
```

```python
import jax
import jax.numpy as jnp
from jax import lax
from jax.experimental import pallas as pl
from jax.experimental.pallas import tpu as pltpu
from jax.sharding import PartitionSpec as P

E = 256
WCOL = 64
BLK = 128
RANK = 256
NEAR = 16
BLK_DEV = 16
PTS = BLK_DEV * BLK
PACK = PTS + BLK_DEV * 32
NODE = RANK + WCOL
LOG2E = 1.4426950408889634
DOT_SCALE = 4.0 * LOG2E
NORM_SCALE = 2.0 * LOG2E
DEAD = 1e30
STEP = 4
F32 = jnp.float32
BF16 = jnp.bfloat16
NT = (((1,), (1,)), ((), ()))


def prep_body(pts, wts, ewts, idx, y_out, l0_out, l12_out):
    y_out[0:PTS, :] = pts[...]
    for b in range(BLK_DEV):
        w = wts[:, b * BLK : (b + 1) * BLK]
        row = PTS + b * 32
        y_out[row : row + 32, 0:BLK] = w[0:32]
        y_out[row : row + 32, BLK:E] = w[32:64]

    def node(r, first, size, out, slot):
        iota = lax.broadcasted_iota(jnp.int32, (RANK, size), 1)
        pick = jnp.where(iota == idx[:, r : r + 1] - first, 1.0, 0.0).astype(BF16)
        rows = lax.dot_general(pick, pts[first : first + size, :], (((1,), (0,)), ((), ())), preferred_element_type=F32)
        out[slot * NODE : slot * NODE + RANK, :] = rows.astype(BF16)
        out[slot * NODE + RANK : (slot + 1) * NODE, :] = ewts[r]

    node(4, 0, 1024, l12_out, 0)
    node(5, 1024, 1024, l12_out, 1)
    node(6, 0, 2048, l12_out, 2)
    for r in range(4):
        node(r, r * 512, 512, l0_out, r)


def prep(points, weights_t, equiv_t, skel_t):
    return pl.pallas_call(
        prep_body,
        out_shape=(
            jax.ShapeDtypeStruct((PACK, E), BF16),
            jax.ShapeDtypeStruct((4 * NODE, E), BF16),
            jax.ShapeDtypeStruct((3 * NODE, E), BF16),
        ),
        cost_estimate=pl.CostEstimate(flops=10**9, bytes_accessed=8 * 10**6, transcendentals=0),
        name="prep",
    )(points, weights_t, equiv_t, skel_t)


def row_norms(x):
    v = x.astype(F32)
    sq = v * v
    half = sq[:, 0:128] + sq[:, 128:256]
    parts = [jnp.sum(half[i : i + 128].T, axis=0, keepdims=True) for i in range(0, x.shape[0], 128)]
    row = parts[0] if len(parts) == 1 else jnp.concatenate(parts, axis=1)
    return row * NORM_SCALE


def column_of(row):
    col = jnp.broadcast_to(row, (128, 128)).T
    return jnp.concatenate([col, col], axis=1)


def tile(x, col, src, src_row, wt):
    dot = lax.dot_general(x, src, NT, preferred_element_type=F32)
    k = jnp.exp2(dot * DOT_SCALE - col - src_row).astype(BF16)
    return lax.dot_general(wt, k, NT, preferred_element_type=F32)


def near_body(inv, near, *refs):
    pieces = refs[:8]
    x_out, norm_out, near_out, xs, sems, out_sems = refs[8:]

    def load(k):
        return pltpu.make_async_copy(pieces[k], xs.at[pl.ds(k * PACK, PACK), :], sems.at[k])

    def store(k):
        return pltpu.make_async_copy(xs.at[pl.ds(k * PACK, PTS), :], x_out.at[k], out_sems.at[k])

    for k in range(8):
        load(k).start()
    for k in range(8):
        load(k).wait()
        store(k).start()

        def norms(q, carry, k=k):
            for u in range(4):
                i = q * 4 + u
                x = xs[pl.ds(pl.multiple_of(k * PACK + i * BLK, BLK), BLK), :]
                norm_out[pl.ds(k * BLK_DEV + i, 1), :] = row_norms(x)
            return carry

        lax.fori_loop(0, BLK_DEV // 4, norms, 0)

    def block(i, carry):
        x = xs[pl.ds(pl.multiple_of(i * BLK, BLK), BLK), :]
        col = column_of(norm_out[pl.ds(i, 1), :])
        acc = None
        for pair in range(NEAR // 2):
            srcs, rows, wts = [], [], []
            for s in range(2):
                v = near[i * NEAR + pair * 2 + s]
                j = jnp.maximum(v, 0)
                k = inv[j // BLK_DEV]
                i2 = j % BLK_DEV
                srcs.append(xs[pl.ds(pl.multiple_of(k * PACK + i2 * BLK, BLK), BLK), :])
                bias = jnp.where(v >= 0, 0.0, DEAD).astype(F32)
                rows.append(norm_out[pl.ds(k * BLK_DEV + i2, 1), :] + bias)
                w = xs[pl.ds(pl.multiple_of(k * PACK + PTS + i2 * 32, 32), 32), :]
                wts.append(jnp.concatenate([w[:, 0:128], w[:, 128:256]], axis=0))
            part = tile(x, col, jnp.concatenate(srcs, axis=0), jnp.concatenate(rows, axis=1), jnp.concatenate(wts, axis=1))
            acc = part if acc is None else acc + part
        near_out[i] = acc
        return carry

    lax.fori_loop(0, BLK_DEV, block, 0)
    for k in range(8):
        store(k).wait()


def near_call(inv, near_list, pieces):
    anys = pl.BlockSpec(memory_space=pl.ANY)
    vm = pl.BlockSpec(memory_space=pltpu.VMEM)
    return pl.pallas_call(
        near_body,
        grid_spec=pltpu.PrefetchScalarGridSpec(
            num_scalar_prefetch=2,
            grid=(),
            in_specs=[anys] * 8,
            out_specs=(anys, vm, vm),
            scratch_shapes=[
                pltpu.VMEM((8 * PACK, E), BF16),
                pltpu.SemaphoreType.DMA((8,)),
                pltpu.SemaphoreType.DMA((8,)),
            ],
        ),
        out_shape=(
            jax.ShapeDtypeStruct((8, PTS, E), BF16),
            jax.ShapeDtypeStruct((8 * BLK_DEV, BLK), F32),
            jax.ShapeDtypeStruct((BLK_DEV, WCOL, BLK), F32),
        ),
        cost_estimate=pl.CostEstimate(flops=6 * 10**9, bytes_accessed=20 * 10**6, transcendentals=4 * 10**6),
        name="near",
    )(inv, near_list, *pieces)


def far_call(name, slots, far, x_all, norms, panel, places, acc):
    levels = len(places)
    panel_nodes = panel.shape[0] // NODE
    steps = 8 * BLK_DEV // STEP
    per_slot = BLK_DEV // STEP

    def body(slots, far, *refs):
        if acc is None:
            x_ref, norm_ref, panel_hbm, out_ref, pan, node_norms, sem = refs
        else:
            x_ref, norm_ref, panel_hbm, acc_ref, out_ref, pan, node_norms, sem = refs
        step = pl.program_id(0)

        @pl.when(step == 0)
        def _():
            copy = pltpu.make_async_copy(panel_hbm, pan, sem)
            copy.start()
            copy.wait()

            def norms_of(q, carry):
                for u in range(4):
                    n = q * 4 + u
                    x = pan[pl.ds(pl.multiple_of(n * NODE, NODE), RANK), :]
                    node_norms[pl.ds(n, 1), :] = row_norms(x)
                return carry

            lax.fori_loop(0, panel_nodes // 4, norms_of, 0)

        k = step // per_slot
        first = (step % per_slot) * STEP
        for u in range(STEP):
            x = x_ref[0, u * BLK : (u + 1) * BLK, :]
            col = column_of(norm_ref[pl.ds(step * STEP + u, 1), :])
            total = None if acc is None else acc_ref[0, u]
            for level in range(levels):
                v = far[(slots[k] * BLK_DEV + first + u) * levels + level]
                n = places[level](jnp.maximum(v, 0))
                row = pl.multiple_of(n * NODE, NODE)
                bias = jnp.where(v >= 0, 0.0, DEAD).astype(F32)
                part = tile(
                    x,
                    col,
                    pan[pl.ds(row, RANK), :],
                    node_norms[pl.ds(n, 1), :] + bias,
                    pan[pl.ds(row + RANK, WCOL), :],
                )
                total = part if total is None else total + part
            out_ref[0, u] = total

    blocked = pl.BlockSpec((1, STEP, WCOL, BLK), lambda s, *_: (s // per_slot, s % per_slot, 0, 0))
    in_specs = [
        pl.BlockSpec((1, STEP * BLK, E), lambda s, *_: (s // per_slot, s % per_slot, 0)),
        pl.BlockSpec((8 * BLK_DEV, BLK), lambda s, *_: (0, 0)),
        pl.BlockSpec(memory_space=pl.ANY),
    ]
    operands = [x_all, norms, panel]
    if acc is not None:
        in_specs.append(blocked)
        operands.append(acc)
    return pl.pallas_call(
        body,
        grid_spec=pltpu.PrefetchScalarGridSpec(
            num_scalar_prefetch=2,
            grid=(steps,),
            in_specs=in_specs,
            out_specs=blocked,
            scratch_shapes=[
                pltpu.VMEM(panel.shape, BF16),
                pltpu.VMEM((panel_nodes, RANK), F32),
                pltpu.SemaphoreType.DMA,
            ],
        ),
        out_shape=jax.ShapeDtypeStruct((8, BLK_DEV, WCOL, BLK), F32),
        cost_estimate=pl.CostEstimate(
            flops=levels * 5 * 10**9, bytes_accessed=25 * 10**6, transcendentals=levels * 4 * 10**6
        ),
        name=name,
    )(slots, far, *operands)


def shards(points, weights, near_list, far_list, skel_index, equiv_weights):
    src_index = lax.axis_index("src")
    y_size = lax.axis_size("src") // 2

    def along_y(d):
        return [(s, ((s // 2 + d) % y_size) * 2 + s % 2) for s in range(2 * y_size)]

    partner = [(s, s ^ 1) for s in range(2 * y_size)]

    def shift(v, d):
        return lax.ppermute(v, "src", along_y(d))

    def swap(v):
        return lax.ppermute(v, "src", partner)

    y, core = src_index // 2, src_index % 2
    ys = [(y + d) % y_size for d in (0, -1, 1, 2)]
    slots = jnp.stack([ys[d] * 2 + (core ^ f) for f in range(2) for d in range(4)])
    inv = jnp.sum(jnp.where(slots[:, None] == jnp.arange(8)[None, :], jnp.arange(8)[:, None], 0), axis=0)
    slots, inv = slots.astype(jnp.int32), inv.astype(jnp.int32)

    pack, l0, l12 = prep(points, weights.T, jnp.swapaxes(equiv_weights, 1, 2), skel_index.T)
    mine = [pack, shift(pack, 1), shift(pack, -1), shift(pack, 2)]
    pieces = mine + [swap(v) for v in mine]
    panel12 = lax.all_gather(l12, "tgt", axis=0, tiled=True)
    panel0 = lax.all_gather(l0, "tgt", axis=0, tiled=True)

    x_all, norms, near_sum = near_call(inv, near_list.reshape(-1), pieces)
    far = far_list[:, :, 0]
    places12 = (lambda v: (v // 2) * 3 + v % 2, lambda v: v * 3 + 2)
    far12 = far_call("far12", slots, far[:, 1:].reshape(-1), x_all, norms, panel12, places12, None)
    total = far_call("far0", slots, far[:, 0].reshape(-1), x_all, norms, panel0, (lambda v: v,), far12)

    chip = total[0:4] + swap(total[4:8].astype(BF16)).astype(F32)
    got = [
        shift(chip[1].astype(BF16), -1),
        shift(chip[2].astype(BF16), 1),
        shift(chip[3].astype(BF16), 2),
    ]
    out = near_sum + chip[0]
    for g in got:
        out = out + g.astype(F32)
    return out.transpose(0, 2, 1).reshape(PTS, WCOL)


def solution(mesh):
    in_specs = (
        P(("tgt", "src"), None),
        P(("tgt", "src"), None),
        P(("tgt", "src"), None),
        P("tgt", None, "src"),
        P(("tgt", "src"), None),
        P(("tgt", "src"), None, None),
    )
    out_specs = P(("tgt", "src"), None)
    return jax.shard_map(shards, mesh=mesh, in_specs=in_specs, out_specs=out_specs, check_vma=False)
```

```python
import jax
import jax.numpy as jnp
from jax import lax
from jax.experimental import pallas as pl
from jax.experimental.pallas import tpu as pltpu
from jax.sharding import PartitionSpec as P

E = 256
WCOL = 64
BLK = 128
RANK = 256
NEAR = 16
BLK_DEV = 16
PTS = BLK_DEV * BLK
PACK = PTS + BLK_DEV * 32
NODE = RANK + WCOL
HALF = 3 * NODE // 2
LOG2E = 1.4426950408889634
DOT_SCALE = 4.0 * LOG2E
NORM_SCALE = 2.0 * LOG2E
DEAD = 1e30
F32 = jnp.float32
BF16 = jnp.bfloat16
NT = (((1,), (1,)), ((), ()))


def prep_body(pts, wts, ewts, idx, y_out, l0_out, half_a, half_b):
    def node(r, first, size):
        iota = lax.broadcasted_iota(jnp.int32, (RANK, size), 1)
        pick = jnp.where(iota == idx[:, r : r + 1] - first, 1.0, 0.0).astype(BF16)
        rows = lax.dot_general(pick, pts[first : first + size, :], (((1,), (0,)), ((), ())), preferred_element_type=F32)
        return rows.astype(BF16)

    half_a[0:RANK, :] = node(4, 0, 1024)
    half_a[RANK:NODE, :] = ewts[4]
    rows = node(5, 1024, 1024)
    cut = HALF - NODE
    half_a[NODE:HALF, :] = rows[0:cut]
    half_b[0 : RANK - cut, :] = rows[cut:RANK]
    half_b[RANK - cut : NODE - cut, :] = ewts[5]
    half_b[NODE - cut : HALF - WCOL, :] = node(6, 0, 2048)
    half_b[HALF - WCOL : HALF, :] = ewts[6]
    for r in range(4):
        l0_out[r * NODE : r * NODE + RANK, :] = node(r, r * 512, 512)
        l0_out[r * NODE + RANK : (r + 1) * NODE, :] = ewts[r]
    y_out[0:PTS, :] = pts[...]
    for b in range(BLK_DEV):
        w = wts[:, b * BLK : (b + 1) * BLK]
        row = PTS + b * 32
        y_out[row : row + 32, 0:BLK] = w[0:32]
        y_out[row : row + 32, BLK:E] = w[32:64]


def prep(points, weights_t, equiv_t, skel_t):
    return pl.pallas_call(
        prep_body,
        out_shape=(
            jax.ShapeDtypeStruct((PACK, E), BF16),
            jax.ShapeDtypeStruct((4 * NODE, E), BF16),
            jax.ShapeDtypeStruct((HALF, E), BF16),
            jax.ShapeDtypeStruct((HALF, E), BF16),
        ),
        cost_estimate=pl.CostEstimate(flops=10**9, bytes_accessed=8 * 10**6, transcendentals=0),
        name="prep",
    )(points, weights_t, equiv_t, skel_t)


def row_norms(x):
    v = x.astype(F32)
    sq = v * v
    half = sq[:, 0:128] + sq[:, 128:256]
    parts = [jnp.sum(half[i : i + 128].T, axis=0, keepdims=True) for i in range(0, x.shape[0], 128)]
    row = parts[0] if len(parts) == 1 else jnp.concatenate(parts, axis=1)
    return row * NORM_SCALE


def column_of(row):
    col = jnp.broadcast_to(row, (128, 128)).T
    return jnp.concatenate([col, col], axis=1)


def tile(x, col, src, src_row, wt):
    dot = lax.dot_general(x, src, NT, preferred_element_type=F32)
    k = jnp.exp2(dot * DOT_SCALE - col - src_row).astype(BF16)
    return lax.dot_general(wt, k, NT, preferred_element_type=F32)


def near_body(inv, near, *refs):
    pieces = refs[:8]
    x_out, norm_out, near_out, xs, sems, out_sems = refs[8:]

    def load(k):
        return pltpu.make_async_copy(pieces[k], xs.at[pl.ds(k * PACK, PACK), :], sems.at[k])

    def store(k):
        return pltpu.make_async_copy(xs.at[pl.ds(k * PACK, PTS), :], x_out.at[k], out_sems.at[k])

    for k in range(8):
        load(k).start()
    for k in range(8):
        load(k).wait()
        store(k).start()

        def norms(q, carry, k=k):
            for u in range(4):
                i = q * 4 + u
                x = xs[pl.ds(pl.multiple_of(k * PACK + i * BLK, BLK), BLK), :]
                norm_out[pl.ds(k * BLK_DEV + i, 1), :] = row_norms(x)
            return carry

        lax.fori_loop(0, BLK_DEV // 4, norms, 0)

    def block(i, carry):
        x = xs[pl.ds(pl.multiple_of(i * BLK, BLK), BLK), :]
        col = column_of(norm_out[pl.ds(i, 1), :])
        acc = None
        for pair in range(NEAR // 2):
            srcs, rows, wts = [], [], []
            for s in range(2):
                v = near[i * NEAR + pair * 2 + s]
                j = jnp.maximum(v, 0)
                k = inv[j // BLK_DEV]
                i2 = j % BLK_DEV
                srcs.append(xs[pl.ds(pl.multiple_of(k * PACK + i2 * BLK, BLK), BLK), :])
                bias = jnp.where(v >= 0, 0.0, DEAD).astype(F32)
                rows.append(norm_out[pl.ds(k * BLK_DEV + i2, 1), :] + bias)
                w = xs[pl.ds(pl.multiple_of(k * PACK + PTS + i2 * 32, 32), 32), :]
                wts.append(jnp.concatenate([w[:, 0:128], w[:, 128:256]], axis=0))
            part = tile(x, col, jnp.concatenate(srcs, axis=0), jnp.concatenate(rows, axis=1), jnp.concatenate(wts, axis=1))
            acc = part if acc is None else acc + part
        near_out[i] = acc
        return carry

    lax.fori_loop(0, BLK_DEV, block, 0)
    for k in range(8):
        store(k).wait()


def near_call(inv, near_list, pieces):
    anys = pl.BlockSpec(memory_space=pl.ANY)
    vm = pl.BlockSpec(memory_space=pltpu.VMEM)
    return pl.pallas_call(
        near_body,
        grid_spec=pltpu.PrefetchScalarGridSpec(
            num_scalar_prefetch=2,
            grid=(),
            in_specs=[anys] * 8,
            out_specs=(anys, vm, vm),
            scratch_shapes=[
                pltpu.VMEM((8 * PACK, E), BF16),
                pltpu.SemaphoreType.DMA((8,)),
                pltpu.SemaphoreType.DMA((8,)),
            ],
        ),
        out_shape=(
            jax.ShapeDtypeStruct((8, PTS, E), BF16),
            jax.ShapeDtypeStruct((8 * BLK_DEV, BLK), F32),
            jax.ShapeDtypeStruct((BLK_DEV, WCOL, BLK), F32),
        ),
        cost_estimate=pl.CostEstimate(flops=6 * 10**9, bytes_accessed=20 * 10**6, transcendentals=4 * 10**6),
        name="near",
    )(inv, near_list, *pieces)


def far_call(name, slots, owners, far, x_all, norms, panels, layout, nodes, places, group):
    levels = len(places)
    count = len(panels)

    def body(slots, owners, far, x_hbm, norm_ref, *refs):
        sources = refs[:count]
        out_hbm, xs, pan, node_norms, out_v, s0, s1, psem, xsem, osem = refs[count:]
        panel_copies = [
            pltpu.make_async_copy(sources[p].at[pl.ds(a, r), :], pan.at[pl.ds(place(owners), r), :], psem.at[i])
            for i, (p, a, r, place) in enumerate(layout)
        ]
        x_copies = [
            pltpu.make_async_copy(x_hbm.at[k], xs.at[pl.ds(k * PTS, PTS), :], xsem.at[k]) for k in range(8)
        ]
        out_copies = [pltpu.make_async_copy(out_v.at[k], out_hbm.at[k], osem.at[k]) for k in range(8)]
        for copy in panel_copies + x_copies:
            copy.start()
        for copy in panel_copies:
            copy.wait()

        def norms_of(q, carry):
            for u in range(4):
                n = q * 4 + u
                x = pan[pl.ds(pl.multiple_of(n * NODE, NODE), RANK), :]
                node_norms[pl.ds(n, 1), :] = row_norms(x)
            return carry

        lax.fori_loop(0, nodes // 4, norms_of, 0)

        def entry(b, level):
            v = far[(slots[b // BLK_DEV] * BLK_DEV + b % BLK_DEV) * levels + level]
            n = places[level](jnp.maximum(v, 0))
            return v, n, pl.multiple_of(n * NODE, NODE)

        def dots(b0, s_ref):
            for u in range(group):
                x = xs[pl.ds(pl.multiple_of((b0 + u) * BLK, BLK), BLK), :]
                col = column_of(norm_ref[pl.ds(b0 + u, 1), :])
                for level in range(levels):
                    _, _, row = entry(b0 + u, level)
                    dot = lax.dot_general(x, pan[pl.ds(row, RANK), :], NT, preferred_element_type=F32)
                    s_ref[u * levels + level] = dot * DOT_SCALE - col

        def finish(b0, s_ref):
            for u in range(group):
                b = b0 + u
                total = None
                for level in range(levels):
                    v, n, row = entry(b, level)
                    bias = jnp.where(v >= 0, 0.0, DEAD).astype(F32)
                    src_row = node_norms[pl.ds(n, 1), :] + bias
                    k = jnp.exp2(s_ref[u * levels + level] - src_row).astype(BF16)
                    wt = pan[pl.ds(row + RANK, WCOL), :]
                    part = lax.dot_general(wt, k, NT, preferred_element_type=F32)
                    total = part if total is None else total + part
                out_v[b // BLK_DEV, b % BLK_DEV] = total

        last = 8 * BLK_DEV - group
        x_copies[0].wait()
        dots(0, s0)
        for k in range(8):
            if k < 7:
                x_copies[k + 1].wait()

            def pair(j, carry, k=k):
                b = k * BLK_DEV + j * 2 * group
                dots(b + group, s1)
                finish(b, s0)
                dots(jnp.minimum(b + 2 * group, last), s0)
                finish(b + group, s1)
                return carry

            lax.fori_loop(0, BLK_DEV // (2 * group), pair, 0)
            out_copies[k].start()
        for copy in out_copies:
            copy.wait()

    anys = pl.BlockSpec(memory_space=pl.ANY)
    return pl.pallas_call(
        body,
        grid_spec=pltpu.PrefetchScalarGridSpec(
            num_scalar_prefetch=3,
            grid=(),
            in_specs=[anys, pl.BlockSpec(memory_space=pltpu.VMEM)] + [anys] * count,
            out_specs=anys,
            scratch_shapes=[
                pltpu.VMEM((8 * PTS, E), BF16),
                pltpu.VMEM((nodes * NODE, E), BF16),
                pltpu.VMEM((nodes, RANK), F32),
                pltpu.VMEM((8, BLK_DEV, WCOL, BLK), F32),
                pltpu.VMEM((group * levels, BLK, RANK), F32),
                pltpu.VMEM((group * levels, BLK, RANK), F32),
                pltpu.SemaphoreType.DMA((len(layout),)),
                pltpu.SemaphoreType.DMA((8,)),
                pltpu.SemaphoreType.DMA((8,)),
            ],
        ),
        out_shape=jax.ShapeDtypeStruct((8, BLK_DEV, WCOL, BLK), F32),
        cost_estimate=pl.CostEstimate(
            flops=levels * 8 * 10**9, bytes_accessed=25 * 10**6, transcendentals=levels * 4 * 10**6
        ),
        name=name,
    )(slots, owners, far, x_all, norms, *panels)


def shards(points, weights, near_list, far_list, skel_index, equiv_weights):
    src_index = lax.axis_index("src")
    y_size = lax.axis_size("src") // 2

    def along_y(d):
        return [(s, ((s // 2 + d) % y_size) * 2 + s % 2) for s in range(2 * y_size)]

    partner = [(s, s ^ 1) for s in range(2 * y_size)]

    def shift(v, d):
        return lax.ppermute(v, "src", along_y(d))

    def swap(v):
        return lax.ppermute(v, "src", partner)

    y, core = src_index // 2, src_index % 2
    ys = [(y + d) % y_size for d in (0, -1, 1, 2)]
    slots = jnp.stack([ys[d] * 2 + (core ^ f) for f in range(2) for d in range(4)])
    inv = jnp.sum(jnp.where(slots[:, None] == jnp.arange(8)[None, :], jnp.arange(8)[:, None], 0), axis=0)
    slots, inv = slots.astype(jnp.int32), inv.astype(jnp.int32)

    def along_z(d):
        return [(t, ((t // 4 + d) % 4) * 4 + t % 4) for t in range(16)]

    def along_x(d):
        return [(t, (t // 4) * 4 + (t % 4 + d) % 4) for t in range(16)]

    def move(v, pairs):
        return lax.ppermute(v, "tgt", pairs)

    def first_axis(v, along):
        return jnp.concatenate([v, move(v, along(1)), move(v, along(-1)), move(v, along(2))], axis=0)

    def second_axis(v, along):
        n = v.shape[0] // 2
        up, down = move(v, along(1)), move(v, along(-1))
        return [v, up, down, move(up[:n], along(1)), move(down[n:], along(-1))]

    tgt_index = lax.axis_index("tgt")
    offsets = jnp.array([0, 3, 1, 2], jnp.int32)
    zs, xs = (tgt_index // 4 + offsets) % 4, (tgt_index % 4 + offsets) % 4
    owners = (zs[:, None] * 4 + xs[None, :]).reshape(-1).astype(jnp.int32)

    pack, l0, half_a, half_b = prep(points, weights.T, jnp.swapaxes(equiv_weights, 1, 2), skel_index.T)
    panel0 = lax.all_gather(l0, "tgt", axis=0, tiled=True)
    panels12 = second_axis(first_axis(half_a, along_z), along_x) + second_axis(first_axis(half_b, along_x), along_z)
    mine = [pack, shift(pack, 1), shift(pack, -1), shift(pack, 2)]
    pieces = mine + [swap(v) for v in mine]

    layout12 = []
    for half in range(2):
        for far_step in range(4):
            for near_step in range(4):
                panel, row = (far_step, near_step) if far_step < 3 else (3 + near_step // 2, near_step % 2)
                owner = near_step * 4 + far_step if half == 0 else far_step * 4 + near_step
                layout12.append(
                    (
                        half * 5 + panel,
                        row * HALF,
                        HALF,
                        lambda o, owner=owner, half=half: pl.multiple_of(o[owner] * (2 * HALF) + half * HALF, 32),
                    )
                )

    x_all, norms, near_sum = near_call(inv, near_list.reshape(-1), pieces)
    far = far_list[:, :, 0]
    places12 = (lambda v: (v // 2) * 3 + v % 2, lambda v: v * 3 + 2)
    far12 = far_call("far12", slots, owners, far[:, 1:].reshape(-1), x_all, norms, panels12, layout12, 48, places12, 4)
    layout0 = [(0, i * 4 * NODE, 4 * NODE, lambda o, i=i: i * 4 * NODE) for i in range(16)]
    far0 = far_call("far0", slots, owners, far[:, 0].reshape(-1), x_all, norms, [panel0], layout0, 64, (lambda v: v,), 4)
    total = far12 + far0

    chip = total[0:4] + swap(total[4:8].astype(BF16)).astype(F32)
    got = [
        shift(chip[1].astype(BF16), -1),
        shift(chip[2].astype(BF16), 1),
        shift(chip[3].astype(BF16), 2),
    ]
    out = near_sum + chip[0]
    for g in got:
        out = out + g.astype(F32)
    return out.transpose(0, 2, 1).reshape(PTS, WCOL)


def solution(mesh):
    in_specs = (
        P(("tgt", "src"), None),
        P(("tgt", "src"), None),
        P(("tgt", "src"), None),
        P("tgt", None, "src"),
        P(("tgt", "src"), None),
        P(("tgt", "src"), None, None),
    )
    out_specs = P(("tgt", "src"), None)
    return jax.shard_map(shards, mesh=mesh, in_specs=in_specs, out_specs=out_specs, check_vma=False)
```

```python
import jax
import jax.numpy as jnp
from jax import lax
from jax.experimental import pallas as pl
from jax.experimental.pallas import tpu as pltpu
from jax.sharding import PartitionSpec as P

E = 256
WCOL = 64
BLK = 128
RANK = 256
NEAR = 16
LEVELS = 3
BLK_DEV = 16
NODE_DEV = 7
PTS = BLK_DEV * BLK
WROWS = BLK_DEV * 32 + 32
PACK = PTS + WROWS
NODE = RANK + WCOL
DATA = NODE_DEV * NODE // 2
HALF = DATA + 16
BLOCKS = 8 * BLK_DEV
LOG2E = 1.4426950408889634
DOT_SCALE = 4.0 * LOG2E
NORM_SCALE = 2.0 * LOG2E
DEAD = 1e30
GROUP = 4
SLACK = 3 * GROUP
F32 = jnp.float32
BF16 = jnp.bfloat16
NT = (((1,), (1,)), ((), ()))


def row_norms(x):
    v = x.astype(F32)
    sq = v * v
    half = sq[:, 0:128] + sq[:, 128:256]
    parts = [jnp.sum(half[i : i + 128].T, axis=0, keepdims=True) for i in range(0, x.shape[0], 128)]
    row = parts[0] if len(parts) == 1 else jnp.concatenate(parts, axis=1)
    return row * NORM_SCALE


def column_of(row, copies=2):
    col = jnp.broadcast_to(row, (128, 128)).T
    return jnp.concatenate([col] * copies, axis=1)


def relative(there, here):
    d = (there - here) & 3
    return jnp.where(d == 0, 0, jnp.where(d == 3, 1, d + 1))


def three_parts(v):
    hi = v.astype(BF16).astype(F32)
    mid = (v - hi).astype(BF16).astype(F32)
    return hi, mid, v - hi - mid


def prep_body(pts, wts, ewts, idx, y_out, half_a, half_b, norms):
    def node(r, first, size):
        parts = []
        for c in range(0, RANK, 128):
            want = column_of(idx[r : r + 1, c : c + 128].astype(F32), size // 128)
            iota = lax.broadcasted_iota(jnp.int32, (128, size), 1).astype(F32)
            pick = jnp.where(iota == want - first, 1.0, 0.0).astype(BF16)
            rows = lax.dot_general(
                pick, pts[first : first + size, :], (((1,), (0,)), ((), ())), preferred_element_type=F32
            )
            parts.append(rows.astype(BF16))
        rows = jnp.concatenate(parts, axis=0)
        for c, part in enumerate(three_parts(row_norms(rows))):
            row = (16 if r >= 3 else 0) + c * 4 + (r - 3 if r >= 3 else r)
            norms[row : row + 1, :] = part
        return rows

    norms[...] = jnp.zeros((32, E), F32)
    cut = DATA - 3 * NODE
    for r in range(3):
        half_a[r * NODE : r * NODE + RANK, :] = node(r, r * 512, 512)
        half_a[r * NODE + RANK : (r + 1) * NODE, :] = ewts[r]
    rows = node(3, 3 * 512, 512)
    half_a[3 * NODE : DATA, :] = rows[0:cut]
    half_b[0 : RANK - cut, :] = rows[cut:RANK]
    half_b[RANK - cut : NODE - cut, :] = ewts[3]
    for r, first, size in ((4, 0, 1024), (5, 1024, 1024), (6, 0, 2048)):
        row = r * NODE - DATA
        half_b[row : row + RANK, :] = node(r, first, size)
        half_b[row + RANK : row + NODE, :] = ewts[r]
    half_a[DATA:HALF, :] = norms[0:16, :].astype(BF16)
    half_b[DATA:HALF, :] = norms[16:32, :].astype(BF16)
    y_out[0:PTS, :] = pts[...]
    for b in range(BLK_DEV):
        w = wts[:, b * BLK : (b + 1) * BLK]
        row = PTS + b * 32
        y_out[row : row + 32, 0:BLK] = w[0:32]
        y_out[row : row + 32, BLK:E] = w[32:64]
        for c, part in enumerate(three_parts(row_norms(pts[b * BLK : (b + 1) * BLK, :]))):
            at = b + c // 2 * 16
            norms[at : at + 1, c % 2 * BLK : (c % 2 + 1) * BLK] = part
    norms[16:32, BLK:E] = jnp.zeros((16, BLK), F32)
    y_out[PACK - 32 : PACK, :] = norms[...].astype(BF16)


def prep(points, weights_t, equiv_t, skel_index):
    return pl.pallas_call(
        prep_body,
        out_shape=(
            jax.ShapeDtypeStruct((PACK, E), BF16),
            jax.ShapeDtypeStruct((HALF, E), BF16),
            jax.ShapeDtypeStruct((HALF, E), BF16),
        ),
        scratch_shapes=[pltpu.VMEM((32, E), F32)],
        cost_estimate=pl.CostEstimate(flops=10**9, bytes_accessed=8 * 10**6, transcendentals=0),
        name="prep",
    )(points, weights_t, equiv_t, skel_index)


def run_entries(total, dots, finish, s0, s1, before=None, state=0):
    def pair(j, state):
        first = j * 2 * GROUP
        if before is not None:
            state = before(j, state)
        dots(first + GROUP, s1)
        finish(first, s0)
        dots(first + 2 * GROUP, s0)
        finish(first + GROUP, s1)
        return state

    dots(0, s0)
    return lax.fori_loop(0, (total + 2 * GROUP - 1) // (2 * GROUP), pair, state)


def sorted_entries(far, tgt_index, src_index):
    level = lax.broadcasted_iota(jnp.int32, far.shape, 0)
    b = lax.broadcasted_iota(jnp.int32, far.shape, 1)
    src = b // BLK_DEV
    slot = ((src & 1) ^ (src_index & 1)) * 4 + relative(src // 2, src_index // 2)
    w = jnp.maximum(far, 0)
    owner = w >> (2 - level)
    r = (w & ((4 >> level) - 1)) + jnp.where(level == 0, 0, 2 * level + 2)
    i, j = relative(owner // 4, tgt_index // 4), relative(owner & 3, tgt_index & 3)
    of_i, of_j = jnp.where(i == 3, 2, jnp.minimum(i, 1)), jnp.where(j == 3, 2, jnp.minimum(j, 1))
    cls = jnp.where(r < 3, of_j, jnp.where(r > 3, of_i, jnp.maximum(of_i, of_j)))
    order = [0] * (16 * NODE_DEV)
    for group in range(3):
        for n, (i2, j2, r2) in enumerate(class_nodes(group)):
            order[(i2 * 4 + j2) * NODE_DEV + r2] = n
    place = (i * 4 + j) * NODE_DEV + r
    hit = place[..., None] == jnp.arange(len(order), dtype=jnp.int32)
    node = jnp.sum(jnp.where(hit, jnp.array(order, jnp.int32), 0), axis=-1)
    node = jnp.where(far >= 0, node, level)
    cls = jnp.where(far >= 0, cls, 3).reshape(-1)
    keys = (cls << 14) | ((slot * BLK_DEV + b % BLK_DEV) << 7 | node).reshape(-1)
    rank = jnp.sum((keys[None, :] < keys[:, None]).astype(jnp.int32), axis=1)
    places = jnp.arange(keys.shape[0], dtype=jnp.int32)
    entries = jnp.sum(jnp.where(rank[None, :] == places[:, None], keys[None, :], 0), axis=1)
    starts = jnp.sum((cls[None, :] < jnp.arange(4, dtype=jnp.int32)[:, None]).astype(jnp.int32), axis=1)
    return entries, starts


def class_nodes(group):
    cls = (0, 1, 1, 2)
    grid = [(i, j) for i in range(4) for j in range(4)]
    nodes = [(i, j, r) for i, j in grid if cls[j] == group for r in range(3)]
    nodes += [(i, j, r) for i, j in grid if cls[i] == group for r in range(4, NODE_DEV)]
    return nodes + [(i, j, 3) for i, j in grid if max(cls[i], cls[j]) == group]


def panel_nodes(group):
    return (len(class_nodes(group)) + 3) // 4 * 4


def panel_layout(group):
    cut = DATA - 3 * NODE
    rows, norms = [], []
    for n, (i, j, r) in enumerate(class_nodes(group)):
        if r == 0:
            spans = [(0, 0, 3 * NODE, 0)]
        elif r == 3:
            spans = [(0, DATA - cut, cut, 0), (1, 0, NODE - cut, cut)]
        elif r == 4:
            spans = [(1, NODE - cut, 3 * NODE, 0)]
        else:
            continue
        for half, row, count, place in spans:
            first, second = (i, j) if half == 0 else (j, i)
            rows.append((half, second * 2 + first // 2, (first % 2) * HALF + row, count, n * NODE + place))
        norms.append((half, second * 2 + first // 2, (first % 2) * HALF + DATA, 16, len(norms) * 16))
    return rows, norms


def panel_norms(group, parts, wide, node_norms):
    wide[...] = parts[...].astype(F32)
    k = -1
    for n, (i, j, r) in enumerate(class_nodes(group)):
        if r in (0, 3, 4):
            k += 1
        row = k * 16 + (r if r < 3 else r - 3)
        node_norms[n : n + 1, :] = wide[row : row + 1, :] + wide[row + 4 : row + 5, :] + wide[row + 8 : row + 9, :]


def run_far(group, starts, entries, xs, norm_ref, pan, node_norms, out_v, s0, s1, arrive=None):
    start, end = starts[group], starts[group + 1]

    def entry(e):
        live = start + e < end
        code = entries[jnp.minimum(start + e, BLOCKS * LEVELS - 1)]
        b = jnp.where(live, (code >> 7) & 127, BLOCKS)
        return b, jnp.where(live, code & 127, 0)

    def dots(first, s_ref):
        for u in range(GROUP):
            b, n = entry(first + u)
            b = jnp.minimum(b, BLOCKS - 1)
            x = xs[pl.ds(pl.multiple_of(b * BLK, BLK), BLK), :]
            src = pan[pl.ds(pl.multiple_of(n * NODE, NODE), RANK), :]
            dot = lax.dot_general(x, src, NT, preferred_element_type=F32)
            s_ref[u] = dot * DOT_SCALE - column_of(norm_ref[pl.ds(b, 1), :])

    def finish(first, s_ref):
        for u in range(GROUP):
            b, n = entry(first + u)
            k = jnp.exp2(s_ref[u] - node_norms[pl.ds(n, 1), :]).astype(BF16)
            wt = pan[pl.ds(pl.multiple_of(n * NODE, NODE) + RANK, WCOL), :]
            out_v[b] = out_v[b] + lax.dot_general(wt, k, NT, preferred_element_type=F32)

    if arrive is None:
        run_entries(end - start, dots, finish, s0, s1)
        return

    def needed(e):
        return jnp.minimum(entry(e)[0] // BLK_DEV, 7) + 1

    arrived = arrive(0, needed(GROUP - 1))

    def before(j, arrived):
        return arrive(arrived, needed(j * 2 * GROUP + 3 * GROUP - 1))

    arrived = run_entries(end - start, dots, finish, s0, s1, before, arrived)
    arrive(arrived, 8)


def near_call(meta, near_list, starts, entries, pieces, panels, rows, nrows):
    count = len(panels)

    def body(meta, near, starts, entries, *refs):
        pieces, sources, refs = refs[:10], refs[10 : 10 + count], refs[10 + count :]
        x_out, norm_out, near_out, sums_out, *refs = refs
        xs, ws, pan, parts, wide, node_norms, acc, out_v, s0, s1, targets, slots, sems, wsem, psem, out_sems = refs
        y, core = meta[1] // 2, meta[1] & 1

        def store(k):
            return pltpu.make_async_copy(xs.at[pl.ds(k * PTS, PTS), :], x_out.at[k], out_sems.at[k])

        loads, cut = [], PACK // 2
        for k in range(8):
            p = k // 4 * 5 + k % 4
            spans = [(p, 0, PTS)] if k % 4 < 3 else [(p, 0, cut), (p + 1, cut, PTS - cut)]
            for piece, row, size in spans:
                first = 0 if piece != p + 1 else row - cut
                loads.append(
                    pltpu.make_async_copy(
                        pieces[piece].at[pl.ds(first, size), :], xs.at[pl.ds(k * PTS + row, size), :], sems.at[piece]
                    )
                )
            piece, first = (p, PTS) if k % 4 < 3 else (p + 1, PTS - cut)
            loads.append(
                pltpu.make_async_copy(
                    pieces[piece].at[pl.ds(first, WROWS), :], ws.at[pl.ds(k * WROWS, WROWS), :], wsem.at[k]
                )
            )

        panel_copies = [
            pltpu.make_async_copy(sources[p].at[pl.ds(a, r), :], to.at[pl.ds(d, r), :], psem.at[i])
            for i, (to, p, a, r, d) in enumerate([(pan, *item) for item in rows] + [(parts, *item) for item in nrows])
        ]
        for copy in loads:
            copy.start()

        def scan_near(i, n):
            for p in range(NEAR // 2):
                targets[n] = i
                slots[n] = 2 * p
                n = n + jnp.where(near[i, 2 * p] >= 0, 1, 0)
            acc[i] = jnp.zeros((WCOL, BLK), F32)
            return n

        total = lax.fori_loop(0, BLK_DEV, scan_near, 0)
        for i in range(SLACK):
            targets[total + i] = BLK_DEV
            slots[total + i] = 0
        acc[BLK_DEV] = jnp.zeros((WCOL, BLK), F32)

        def clear(b, carry):
            out_v[b] = jnp.zeros((WCOL, BLK), F32)
            return carry

        lax.fori_loop(0, BLOCKS + 1, clear, 0)
        for k in range(8):
            for copy in (loads[k // 4 * 9 + k % 4 * 2 :])[: 3 if k % 4 == 3 else 2]:
                copy.wait()
            store(k).start()

            v = ws[pl.ds(k * WROWS + WROWS - 32, 32), :].astype(F32)
            norm_out[pl.ds(k * BLK_DEV, BLK_DEV), :] = v[0:16, 0:BLK] + v[0:16, BLK:E] + v[16:32, 0:BLK]
        for copy in panel_copies:
            copy.start()

        def source(i, slot):
            v = near[i, slot]
            j = jnp.maximum(v, 0)
            k = (((j // BLK_DEV) & 1) ^ core) * 4 + relative(j // (2 * BLK_DEV), y)
            return v, k, j % BLK_DEV

        def dots(first, s_ref):
            for u in range(GROUP):
                i = jnp.minimum(targets[first + u], BLK_DEV - 1)
                x = xs[pl.ds(pl.multiple_of(i * BLK, BLK), BLK), :]
                srcs, rows = [], []
                for s in range(2):
                    v, k, b = source(i, slots[first + u] + s)
                    srcs.append(xs[pl.ds(pl.multiple_of(k * PTS + b * BLK, BLK), BLK), :])
                    bias = jnp.where(v >= 0, 0.0, DEAD).astype(F32)
                    rows.append(norm_out[pl.ds(k * BLK_DEV + b, 1), :] + bias)
                dot = lax.dot_general(x, jnp.concatenate(srcs, axis=0), NT, preferred_element_type=F32)
                col = column_of(norm_out[pl.ds(i, 1), :])
                s_ref[u] = dot * DOT_SCALE - col - jnp.concatenate(rows, axis=1)

        def finish(first, s_ref):
            for u in range(GROUP):
                target = targets[first + u]
                i = jnp.minimum(target, BLK_DEV - 1)
                wts = []
                for s in range(2):
                    _, k, b = source(i, slots[first + u] + s)
                    w = ws[pl.ds(pl.multiple_of(k * WROWS + b * 32, 32), 32), :]
                    wts.append(jnp.concatenate([w[:, 0:128], w[:, 128:256]], axis=0))
                k = jnp.exp2(s_ref[u]).astype(BF16)
                acc[target] = acc[target] + lax.dot_general(
                    jnp.concatenate(wts, axis=1), k, NT, preferred_element_type=F32
                )

        run_entries(total, dots, finish, s0, s1)
        near_out[...] = acc[0:BLK_DEV]

        for copy in panel_copies:
            copy.wait()
        panel_norms(0, parts, wide, node_norms)

        run_far(0, starts, entries, xs, norm_out, pan, node_norms, out_v, s0, s1)
        result = pltpu.make_async_copy(out_v.at[pl.ds(0, BLOCKS)], sums_out, out_sems.at[8])
        result.start()
        for k in range(8):
            store(k).wait()
        result.wait()

    anys = pl.BlockSpec(memory_space=pl.ANY)
    vm = pl.BlockSpec(memory_space=pltpu.VMEM)
    return pl.pallas_call(
        body,
        grid_spec=pltpu.PrefetchScalarGridSpec(
            num_scalar_prefetch=4,
            grid=(),
            in_specs=[anys] * (10 + count),
            out_specs=[anys, vm, vm, anys],
            scratch_shapes=[
                pltpu.VMEM((8 * PTS, E), BF16),
                pltpu.VMEM((8 * WROWS, E), BF16),
                pltpu.VMEM((panel_nodes(0) * NODE, E), BF16),
                pltpu.VMEM((len(nrows) * 16, E), BF16),
                pltpu.VMEM((len(nrows) * 16, E), F32),
                pltpu.VMEM((panel_nodes(0), RANK), F32),
                pltpu.VMEM((BLK_DEV + 1, WCOL, BLK), F32),
                pltpu.VMEM((BLOCKS + 1, WCOL, BLK), F32),
                pltpu.VMEM((GROUP, BLK, RANK), F32),
                pltpu.VMEM((GROUP, BLK, RANK), F32),
                pltpu.SMEM((BLK_DEV * NEAR // 2 + SLACK,), jnp.int32),
                pltpu.SMEM((BLK_DEV * NEAR // 2 + SLACK,), jnp.int32),
                pltpu.SemaphoreType.DMA((10,)),
                pltpu.SemaphoreType.DMA((8,)),
                pltpu.SemaphoreType.DMA((len(rows) + len(nrows),)),
                pltpu.SemaphoreType.DMA((9,)),
            ],
        ),
        out_shape=[
            jax.ShapeDtypeStruct((8, PTS, E), BF16),
            jax.ShapeDtypeStruct((BLOCKS, BLK), F32),
            jax.ShapeDtypeStruct((BLK_DEV, WCOL, BLK), F32),
            jax.ShapeDtypeStruct((BLOCKS, WCOL, BLK), F32),
        ],
        cost_estimate=pl.CostEstimate(flops=9 * 10**9, bytes_accessed=30 * 10**6, transcendentals=6 * 10**6),
        name="near",
    )(meta, near_list, starts, entries, *pieces, *panels)


def far_call(group, starts, entries, x_all, norms, accs, panels, rows, nrows):
    count, extra = len(panels), len(accs)
    last = extra > 0

    def body(starts, entries, x_hbm, norm_ref, *refs):
        sources, sums, refs = refs[:count], refs[count : count + extra], refs[count + extra :]
        if last:
            keep_hbm, send_hbm, *refs, acc_v, send_v = refs
        else:
            out_hbm, *refs = refs
        out_v, xs, pan, parts, wide, node_norms, s0, s1, psem, xsem, osem = refs
        panel_copies = [
            pltpu.make_async_copy(sources[p].at[pl.ds(a, r), :], to.at[pl.ds(d, r), :], psem.at[i])
            for i, (to, p, a, r, d) in enumerate([(pan, *item) for item in rows] + [(parts, *item) for item in nrows])
        ]
        acc_copies = [pltpu.make_async_copy(sums[i], acc_v.at[i], osem.at[i]) for i in range(extra)]

        def x_copy(k):
            return pltpu.make_async_copy(x_hbm.at[k], xs.at[pl.ds(k * PTS, PTS), :], xsem.at[k])

        for copy in panel_copies + [x_copy(k) for k in range(8)] + acc_copies:
            copy.start()

        def clear(b, carry):
            out_v[b] = jnp.zeros((WCOL, BLK), F32)
            return carry

        lax.fori_loop(0, BLOCKS + 1, clear, 0)
        for copy in panel_copies:
            copy.wait()
        panel_norms(group, parts, wide, node_norms)

        def arrive(done, upto):
            def wait(k, carry):
                x_copy(k).wait()
                return carry

            lax.fori_loop(done, upto, wait, 0)
            return jnp.maximum(done, upto)

        run_far(group, starts, entries, xs, norm_ref, pan, node_norms, out_v, s0, s1, arrive)
        if last:
            for copy in acc_copies:
                copy.wait()

            def merge(b, carry):
                c = BLOCKS // 2 + b
                send_v[b] = (out_v[c] + (acc_v[0, c] + acc_v[1, c])).astype(BF16)
                return carry

            def merge_kept(b, carry):
                out_v[b] = out_v[b] + (acc_v[0, b] + acc_v[1, b])
                return carry

            copies = [
                pltpu.make_async_copy(send_v, send_hbm, osem.at[0]),
                pltpu.make_async_copy(out_v.at[pl.ds(0, BLOCKS // 2)], keep_hbm, osem.at[1]),
            ]
            lax.fori_loop(0, BLOCKS // 2, merge, 0)
            copies[0].start()
            lax.fori_loop(0, BLOCKS // 2, merge_kept, 0)
            copies[1].start()
        else:
            copies = [pltpu.make_async_copy(out_v.at[pl.ds(0, BLOCKS)], out_hbm, osem.at[0])]
            copies[0].start()
        for copy in copies:
            copy.wait()

    anys = pl.BlockSpec(memory_space=pl.ANY)
    sums = (BLOCKS, WCOL, BLK)
    half = (BLOCKS // 2, WCOL, BLK)
    return pl.pallas_call(
        body,
        grid_spec=pltpu.PrefetchScalarGridSpec(
            num_scalar_prefetch=2,
            grid=(),
            in_specs=[anys, pl.BlockSpec(memory_space=pltpu.VMEM)] + [anys] * (count + extra),
            out_specs=(anys, anys) if last else anys,
            scratch_shapes=[
                pltpu.VMEM((BLOCKS + 1, WCOL, BLK), F32),
                pltpu.VMEM((8 * PTS, E), BF16),
                pltpu.VMEM((panel_nodes(group) * NODE, E), BF16),
                pltpu.VMEM((len(nrows) * 16, E), BF16),
                pltpu.VMEM((len(nrows) * 16, E), F32),
                pltpu.VMEM((panel_nodes(group), RANK), F32),
                pltpu.VMEM((GROUP, BLK, RANK), F32),
                pltpu.VMEM((GROUP, BLK, RANK), F32),
                pltpu.SemaphoreType.DMA((len(rows) + len(nrows),)),
                pltpu.SemaphoreType.DMA((8,)),
                pltpu.SemaphoreType.DMA((2,)),
            ]
            + ([pltpu.VMEM((extra, *sums), F32), pltpu.VMEM(half, BF16)] if last else []),
        ),
        out_shape=(jax.ShapeDtypeStruct(half, F32), jax.ShapeDtypeStruct(half, BF16))
        if last
        else jax.ShapeDtypeStruct(sums, F32),
        cost_estimate=pl.CostEstimate(
            flops=(5 if last else 10) * 10**9, bytes_accessed=25 * 10**6, transcendentals=6 * 10**6
        ),
    )(starts, entries, x_all, norms, *panels, *accs)


def shards(points, weights, near_list, far_list, skel_index, equiv_weights):
    def along_y(d):
        return [(s, ((s // 2 + d) % 4) * 2 + s % 2) for s in range(8)]

    def along_z(d):
        return [(t, ((t // 4 + d) % 4) * 4 + t % 4) for t in range(16)]

    def along_x(d):
        return [(t, (t // 4) * 4 + (t % 4 + d) % 4) for t in range(16)]

    partner = [(s, s ^ 1) for s in range(8)]

    def move(v, axis, pairs):
        return lax.ppermute(v, axis, pairs)

    meta = jnp.stack([lax.axis_index("tgt"), lax.axis_index("src")]).astype(jnp.int32)
    entries, starts = sorted_entries(far_list[:, :, 0].T, lax.axis_index("tgt"), lax.axis_index("src"))
    pack, half_a, half_b = prep(points, weights.T, jnp.swapaxes(equiv_weights, 1, 2), skel_index)

    def first_axis(v, along):
        return [v] + [move(v, "tgt", along(d)) for d in (1, -1, 2)]

    def second_axis(v, along):
        low, high = jnp.concatenate(v[:2], axis=0), jnp.concatenate(v[2:], axis=0)
        up0, down1 = move(low, "tgt", along(1)), move(high, "tgt", along(-1))
        up1, down0 = move(high, "tgt", along(1)), move(low, "tgt", along(-1))
        return [low, high, up0, up1, down0, down1, move(up0, "tgt", along(1)), move(down1, "tgt", along(-1))]

    a4 = first_axis(half_a, along_z)
    b4 = first_axis(half_b, along_x)
    panels = second_axis(a4, along_x) + second_axis(b4, along_z)
    up, down = move(pack, "src", along_y(1)), move(pack, "src", along_y(-1))
    cut = PACK // 2
    mine = [pack, up, down, move(up[:cut], "src", along_y(1)), move(down[cut:], "src", along_y(-1))]
    pieces = mine + [move(v, "src", partner) for v in mine]

    def operands(group):
        kinds = panel_layout(group)
        used = sorted({half * 8 + p for items in kinds for half, p, _, _, _ in items})
        copies = [[(used.index(h * 8 + p), a, r, d) for h, p, a, r, d in items] for items in kinds]
        return [panels[u] for u in used], *copies

    x_all, norms, near_sum, sums0 = near_call(meta, near_list, starts, entries, pieces, *operands(0))
    sums1 = far_call(1, starts, entries, x_all, norms, [], *operands(1))
    keep, send = far_call(2, starts, entries, x_all, norms, [sums0, sums1], *operands(2))

    half = (4, BLK_DEV, WCOL, BLK)
    keep, got = keep.reshape(half), move(send, "src", partner).reshape(half)
    out = near_sum + keep[0] + got[0].astype(F32)
    for i, d in ((3, 2), (1, -1), (2, 1)):
        chip = (keep[i] + got[i].astype(F32)).astype(BF16)
        out = out + move(chip, "src", along_y(d)).astype(F32)
    return out.transpose(0, 2, 1).reshape(PTS, WCOL)


def solution(mesh):
    in_specs = (
        P(("tgt", "src"), None),
        P(("tgt", "src"), None),
        P(("tgt", "src"), None),
        P("tgt", None, "src"),
        P(("tgt", "src"), None),
        P(("tgt", "src"), None, None),
    )
    out_specs = P(("tgt", "src"), None)

    return jax.shard_map(shards, mesh=mesh, in_specs=in_specs, out_specs=out_specs, check_vma=False)
```

```python
import jax
import jax.numpy as jnp
from jax import lax
from jax.experimental import pallas as pl
from jax.experimental.pallas import tpu as pltpu
from jax.sharding import PartitionSpec as P

E = 256
WCOL = 64
BLK = 128
RANK = 256
NEAR = 16
LEVELS = 3
BLK_DEV = 16
NODE_DEV = 7
PTS = BLK_DEV * BLK
WROWS = BLK_DEV * 32 + 32
PACK = PTS + WROWS
NODE = RANK + WCOL
DATA = NODE_DEV * NODE // 2
HALF = DATA + 16
BLOCKS = 8 * BLK_DEV
LOG2E = 1.4426950408889634
DOT_SCALE = 4.0 * LOG2E
NORM_SCALE = 2.0 * LOG2E
DEAD = 1e30
GROUP = 4
SLACK = 3 * GROUP
F32 = jnp.float32
BF16 = jnp.bfloat16
NT = (((1,), (1,)), ((), ()))


def row_norms(x):
    v = x.astype(F32)
    sq = v * v
    half = sq[:, 0:128] + sq[:, 128:256]
    parts = [jnp.sum(half[i : i + 128].T, axis=0, keepdims=True) for i in range(0, x.shape[0], 128)]
    row = parts[0] if len(parts) == 1 else jnp.concatenate(parts, axis=1)
    return row * NORM_SCALE


def column_of(row, copies=2):
    col = jnp.broadcast_to(row, (128, 128)).T
    return jnp.concatenate([col] * copies, axis=1)


def relative(there, here):
    d = (there - here) & 3
    return jnp.where(d == 0, 0, jnp.where(d == 3, 1, d + 1))


def three_parts(v):
    hi = v.astype(BF16).astype(F32)
    mid = (v - hi).astype(BF16).astype(F32)
    return hi, mid, v - hi - mid


def prep_body(pts, wts, ewts, idx, y_out, half_a, half_b, norms):
    def node(r, first, size):
        parts = []
        for c in range(0, RANK, 128):
            want = column_of(idx[r : r + 1, c : c + 128].astype(F32), size // 128)
            iota = lax.broadcasted_iota(jnp.int32, (128, size), 1).astype(F32)
            pick = jnp.where(iota == want - first, 1.0, 0.0).astype(BF16)
            rows = lax.dot_general(
                pick, pts[first : first + size, :], (((1,), (0,)), ((), ())), preferred_element_type=F32
            )
            parts.append(rows.astype(BF16))
        rows = jnp.concatenate(parts, axis=0)
        for c, part in enumerate(three_parts(row_norms(rows))):
            row = (16 if r >= 3 else 0) + c * 4 + (r - 3 if r >= 3 else r)
            norms[row : row + 1, :] = part
        return rows

    norms[...] = jnp.zeros((32, E), F32)
    cut = DATA - 3 * NODE
    for r in range(3):
        half_a[r * NODE : r * NODE + RANK, :] = node(r, r * 512, 512)
        half_a[r * NODE + RANK : (r + 1) * NODE, :] = ewts[r]
    rows = node(3, 3 * 512, 512)
    half_a[3 * NODE : DATA, :] = rows[0:cut]
    half_b[0 : RANK - cut, :] = rows[cut:RANK]
    half_b[RANK - cut : NODE - cut, :] = ewts[3]
    for r, first, size in ((4, 0, 1024), (5, 1024, 1024), (6, 0, 2048)):
        row = r * NODE - DATA
        half_b[row : row + RANK, :] = node(r, first, size)
        half_b[row + RANK : row + NODE, :] = ewts[r]
    half_a[DATA:HALF, :] = norms[0:16, :].astype(BF16)
    half_b[DATA:HALF, :] = norms[16:32, :].astype(BF16)
    y_out[0:PTS, :] = pts[...]
    for b in range(BLK_DEV):
        w = wts[:, b * BLK : (b + 1) * BLK]
        row = PTS + b * 32
        y_out[row : row + 32, 0:BLK] = w[0:32]
        y_out[row : row + 32, BLK:E] = w[32:64]
        for c, part in enumerate(three_parts(row_norms(pts[b * BLK : (b + 1) * BLK, :]))):
            at = b + c // 2 * 16
            norms[at : at + 1, c % 2 * BLK : (c % 2 + 1) * BLK] = part
    norms[16:32, BLK:E] = jnp.zeros((16, BLK), F32)
    y_out[PACK - 32 : PACK, :] = norms[...].astype(BF16)


def prep(points, weights_t, equiv_t, skel_index):
    return pl.pallas_call(
        prep_body,
        out_shape=(
            jax.ShapeDtypeStruct((PACK, E), BF16),
            jax.ShapeDtypeStruct((HALF, E), BF16),
            jax.ShapeDtypeStruct((HALF, E), BF16),
        ),
        scratch_shapes=[pltpu.VMEM((32, E), F32)],
        cost_estimate=pl.CostEstimate(flops=10**9, bytes_accessed=8 * 10**6, transcendentals=0),
        name="prep",
    )(points, weights_t, equiv_t, skel_index)


def run_entries(total, dots, finish, s0, s1, before=None, state=0):
    def pair(j, state):
        first = j * 2 * GROUP
        if before is not None:
            state = before(j, state)
        dots(first + GROUP, s1)
        finish(first, s0)
        dots(first + 2 * GROUP, s0)
        finish(first + GROUP, s1)
        return state

    dots(0, s0)
    return lax.fori_loop(0, (total + 2 * GROUP - 1) // (2 * GROUP), pair, state)


def sorted_entries(far, tgt_index, src_index):
    level = lax.broadcasted_iota(jnp.int32, far.shape, 0)
    b = lax.broadcasted_iota(jnp.int32, far.shape, 1)
    src = b // BLK_DEV
    slot = ((src & 1) ^ (src_index & 1)) * 4 + relative(src // 2, src_index // 2)
    w = jnp.maximum(far, 0)
    owner = w >> (2 - level)
    r = (w & ((4 >> level) - 1)) + jnp.where(level == 0, 0, 2 * level + 2)
    i, j = relative(owner // 4, tgt_index // 4), relative(owner & 3, tgt_index & 3)
    of_i, of_j = jnp.where(i == 3, 2, jnp.minimum(i, 1)), jnp.where(j == 3, 2, jnp.minimum(j, 1))
    cls = jnp.where(r < 3, of_j, jnp.where(r > 3, of_i, jnp.maximum(of_i, of_j)))
    order = [0] * (16 * NODE_DEV)
    for group in range(3):
        for n, (i2, j2, r2) in enumerate(class_nodes(group)):
            order[(i2 * 4 + j2) * NODE_DEV + r2] = n
    place = (i * 4 + j) * NODE_DEV + r
    hit = place[..., None] == jnp.arange(len(order), dtype=jnp.int32)
    node = jnp.sum(jnp.where(hit, jnp.array(order, jnp.int32), 0), axis=-1)
    node = jnp.where(far >= 0, node, level)
    cls = jnp.where(far >= 0, cls, 3).reshape(-1)
    keys = (cls << 14) | ((slot * BLK_DEV + b % BLK_DEV) << 7 | node).reshape(-1)
    rank = jnp.sum((keys[None, :] < keys[:, None]).astype(jnp.int32), axis=1)
    places = jnp.arange(keys.shape[0], dtype=jnp.int32)
    entries = jnp.sum(jnp.where(rank[None, :] == places[:, None], keys[None, :], 0), axis=1)
    starts = jnp.sum((cls[None, :] < jnp.arange(4, dtype=jnp.int32)[:, None]).astype(jnp.int32), axis=1)
    return entries, starts


def class_nodes(group):
    cls = (0, 1, 1, 2)
    grid = [(i, j) for i in range(4) for j in range(4)]
    nodes = [(i, j, r) for i, j in grid if cls[j] == group for r in range(3)]
    nodes += [(i, j, r) for i, j in grid if cls[i] == group for r in range(4, NODE_DEV)]
    return nodes + [(i, j, 3) for i, j in grid if max(cls[i], cls[j]) == group]


def panel_nodes(group):
    return (len(class_nodes(group)) + 3) // 4 * 4


def panel_layout(group):
    cut = DATA - 3 * NODE
    rows, norms = [], []
    for n, (i, j, r) in enumerate(class_nodes(group)):
        if r == 0:
            spans = [(0, 0, 3 * NODE, 0)]
        elif r == 3:
            spans = [(0, DATA - cut, cut, 0), (1, 0, NODE - cut, cut)]
        elif r == 4:
            spans = [(1, NODE - cut, 3 * NODE, 0)]
        else:
            continue
        for half, row, count, place in spans:
            first, second = (i, j) if half == 0 else (j, i)
            rows.append((half, second * 2 + first // 2, (first % 2) * HALF + row, count, n * NODE + place))
        norms.append((half, second * 2 + first // 2, (first % 2) * HALF + DATA, 16, len(norms) * 16))
    return rows, norms


def panel_norms(group, parts, wide, node_norms):
    wide[...] = parts[...].astype(F32)
    k = -1
    for n, (i, j, r) in enumerate(class_nodes(group)):
        if r in (0, 3, 4):
            k += 1
        row = k * 16 + (r if r < 3 else r - 3)
        node_norms[n : n + 1, :] = wide[row : row + 1, :] + wide[row + 4 : row + 5, :] + wide[row + 8 : row + 9, :]


def run_far(group, starts, entries, xs, norm_ref, pan, node_norms, out_v, s0, s1, arrive=None):
    start, end = starts[group], starts[group + 1]

    def entry(e):
        live = start + e < end
        code = entries[jnp.minimum(start + e, BLOCKS * LEVELS - 1)]
        b = jnp.where(live, (code >> 7) & 127, BLOCKS)
        return b, jnp.where(live, code & 127, 0)

    def dots(first, s_ref):
        for u in range(GROUP):
            b, n = entry(first + u)
            b = jnp.minimum(b, BLOCKS - 1)
            x = xs[pl.ds(pl.multiple_of(b * BLK, BLK), BLK), :]
            src = pan[pl.ds(pl.multiple_of(n * NODE, NODE), RANK), :]
            dot = lax.dot_general(x, src, NT, preferred_element_type=F32)
            s_ref[u] = dot * DOT_SCALE - column_of(norm_ref[pl.ds(b, 1), :])

    def finish(first, s_ref):
        for u in range(GROUP):
            b, n = entry(first + u)
            k = jnp.exp2(s_ref[u] - node_norms[pl.ds(n, 1), :]).astype(BF16)
            wt = pan[pl.ds(pl.multiple_of(n * NODE, NODE) + RANK, WCOL), :]
            out_v[b] = out_v[b] + lax.dot_general(wt, k, NT, preferred_element_type=F32)

    if arrive is None:
        run_entries(end - start, dots, finish, s0, s1)
        return

    def needed(e):
        return jnp.minimum(entry(e)[0] // BLK_DEV, 7) + 1

    arrived = arrive(0, needed(GROUP - 1))

    def before(j, arrived):
        return arrive(arrived, needed(j * 2 * GROUP + 3 * GROUP - 1))

    arrived = run_entries(end - start, dots, finish, s0, s1, before, arrived)
    arrive(arrived, 8)


def near_call(meta, near_list, starts, entries, pieces, panels, rows, nrows):
    count = len(panels)

    def body(meta, near, starts, entries, *refs):
        pieces, sources, refs = refs[:10], refs[10 : 10 + count], refs[10 + count :]
        x_out, norm_out, near_out, sums_out, *refs = refs
        xs, ws, pan, parts, wide, node_norms, acc, out_v, s0, s1, targets, slots, sems, wsem, psem, out_sems = refs
        y, core = meta[1] // 2, meta[1] & 1

        def store(k):
            return pltpu.make_async_copy(xs.at[pl.ds(k * PTS, PTS), :], x_out.at[k], out_sems.at[k])

        loads, cut = [], PACK // 2
        for k in range(8):
            p = k // 4 * 5 + k % 4
            spans = [(p, 0, PTS)] if k % 4 < 3 else [(p, 0, cut), (p + 1, cut, PTS - cut)]
            for piece, row, size in spans:
                first = 0 if piece != p + 1 else row - cut
                loads.append(
                    pltpu.make_async_copy(
                        pieces[piece].at[pl.ds(first, size), :], xs.at[pl.ds(k * PTS + row, size), :], sems.at[piece]
                    )
                )
            piece, first = (p, PTS) if k % 4 < 3 else (p + 1, PTS - cut)
            loads.append(
                pltpu.make_async_copy(
                    pieces[piece].at[pl.ds(first, WROWS), :], ws.at[pl.ds(k * WROWS, WROWS), :], wsem.at[k]
                )
            )

        panel_copies = [
            pltpu.make_async_copy(sources[p].at[pl.ds(a, r), :], to.at[pl.ds(d, r), :], psem.at[i])
            for i, (to, p, a, r, d) in enumerate([(pan, *item) for item in rows] + [(parts, *item) for item in nrows])
        ]
        for copy in loads:
            copy.start()

        def scan_near(i, n):
            for p in range(NEAR // 2):
                targets[n] = i
                slots[n] = 2 * p
                n = n + jnp.where(near[i, 2 * p] >= 0, 1, 0)
            acc[i] = jnp.zeros((WCOL, BLK), F32)
            return n

        total = lax.fori_loop(0, BLK_DEV, scan_near, 0)
        for i in range(SLACK):
            targets[total + i] = BLK_DEV
            slots[total + i] = 0
        acc[BLK_DEV] = jnp.zeros((WCOL, BLK), F32)

        def clear(b, carry):
            out_v[b] = jnp.zeros((WCOL, BLK), F32)
            return carry

        lax.fori_loop(0, BLOCKS + 1, clear, 0)
        for k in range(8):
            for copy in (loads[k // 4 * 9 + k % 4 * 2 :])[: 3 if k % 4 == 3 else 2]:
                copy.wait()
            store(k).start()

            v = ws[pl.ds(k * WROWS + WROWS - 32, 32), :].astype(F32)
            norm_out[pl.ds(k * BLK_DEV, BLK_DEV), :] = v[0:16, 0:BLK] + v[0:16, BLK:E] + v[16:32, 0:BLK]
        for copy in panel_copies:
            copy.start()

        def source(i, slot):
            v = near[i, slot]
            j = jnp.maximum(v, 0)
            k = (((j // BLK_DEV) & 1) ^ core) * 4 + relative(j // (2 * BLK_DEV), y)
            return v, k, j % BLK_DEV

        def dots(first, s_ref):
            for u in range(GROUP):
                i = jnp.minimum(targets[first + u], BLK_DEV - 1)
                x = xs[pl.ds(pl.multiple_of(i * BLK, BLK), BLK), :]
                srcs, rows = [], []
                for s in range(2):
                    v, k, b = source(i, slots[first + u] + s)
                    srcs.append(xs[pl.ds(pl.multiple_of(k * PTS + b * BLK, BLK), BLK), :])
                    bias = jnp.where(v >= 0, 0.0, DEAD).astype(F32)
                    rows.append(norm_out[pl.ds(k * BLK_DEV + b, 1), :] + bias)
                dot = lax.dot_general(x, jnp.concatenate(srcs, axis=0), NT, preferred_element_type=F32)
                col = column_of(norm_out[pl.ds(i, 1), :])
                s_ref[u] = dot * DOT_SCALE - col - jnp.concatenate(rows, axis=1)

        def finish(first, s_ref):
            for u in range(GROUP):
                target = targets[first + u]
                i = jnp.minimum(target, BLK_DEV - 1)
                wts = []
                for s in range(2):
                    _, k, b = source(i, slots[first + u] + s)
                    w = ws[pl.ds(pl.multiple_of(k * WROWS + b * 32, 32), 32), :]
                    wts.append(jnp.concatenate([w[:, 0:128], w[:, 128:256]], axis=0))
                k = jnp.exp2(s_ref[u]).astype(BF16)
                acc[target] = acc[target] + lax.dot_general(
                    jnp.concatenate(wts, axis=1), k, NT, preferred_element_type=F32
                )

        run_entries(total, dots, finish, s0, s1)
        near_out[...] = acc[0:BLK_DEV]

        for copy in panel_copies:
            copy.wait()
        panel_norms(0, parts, wide, node_norms)

        run_far(0, starts, entries, xs, norm_out, pan, node_norms, out_v, s0, s1)
        result = pltpu.make_async_copy(out_v.at[pl.ds(0, BLOCKS)], sums_out, out_sems.at[8])
        result.start()
        for k in range(8):
            store(k).wait()
        result.wait()

    anys = pl.BlockSpec(memory_space=pltpu.HBM)
    vm = pl.BlockSpec(memory_space=pltpu.VMEM)
    return pl.pallas_call(
        body,
        grid_spec=pltpu.PrefetchScalarGridSpec(
            num_scalar_prefetch=4,
            grid=(),
            in_specs=[anys] * (10 + count),
            out_specs=[anys, vm, vm, anys],
            scratch_shapes=[
                pltpu.VMEM((8 * PTS, E), BF16),
                pltpu.VMEM((8 * WROWS, E), BF16),
                pltpu.VMEM((panel_nodes(0) * NODE, E), BF16),
                pltpu.VMEM((len(nrows) * 16, E), BF16),
                pltpu.VMEM((len(nrows) * 16, E), F32),
                pltpu.VMEM((panel_nodes(0), RANK), F32),
                pltpu.VMEM((BLK_DEV + 1, WCOL, BLK), F32),
                pltpu.VMEM((BLOCKS + 1, WCOL, BLK), F32),
                pltpu.VMEM((GROUP, BLK, RANK), F32),
                pltpu.VMEM((GROUP, BLK, RANK), F32),
                pltpu.SMEM((BLK_DEV * NEAR // 2 + SLACK,), jnp.int32),
                pltpu.SMEM((BLK_DEV * NEAR // 2 + SLACK,), jnp.int32),
                pltpu.SemaphoreType.DMA((10,)),
                pltpu.SemaphoreType.DMA((8,)),
                pltpu.SemaphoreType.DMA((len(rows) + len(nrows),)),
                pltpu.SemaphoreType.DMA((9,)),
            ],
        ),
        out_shape=[
            jax.ShapeDtypeStruct((8, PTS, E), BF16),
            jax.ShapeDtypeStruct((BLOCKS, BLK), F32),
            jax.ShapeDtypeStruct((BLK_DEV, WCOL, BLK), F32),
            jax.ShapeDtypeStruct((BLOCKS, WCOL, BLK), F32),
        ],
        cost_estimate=pl.CostEstimate(flops=9 * 10**9, bytes_accessed=30 * 10**6, transcendentals=6 * 10**6),
        name="near",
    )(meta, near_list, starts, entries, *pieces, *panels)


def far_call(group, starts, entries, x_all, norms, acc, panels, rows, nrows):
    count = len(panels)
    last = group == 2

    def body(starts, entries, x_hbm, norm_ref, *refs):
        sources, acc_hbm, refs = refs[:count], refs[count], refs[count + 1 :]
        if last:
            keep_hbm, send_hbm, *refs, send_v = refs
        else:
            out_hbm, *refs = refs
        out_v, acc_v, xs, pan, parts, wide, node_norms, s0, s1, psem, xsem, osem = refs
        panel_copies = [
            pltpu.make_async_copy(sources[p].at[pl.ds(a, r), :], to.at[pl.ds(d, r), :], psem.at[i])
            for i, (to, p, a, r, d) in enumerate([(pan, *item) for item in rows] + [(parts, *item) for item in nrows])
        ]
        acc_copy = pltpu.make_async_copy(acc_hbm, acc_v, osem.at[0])

        def x_copy(k):
            return pltpu.make_async_copy(x_hbm.at[k], xs.at[pl.ds(k * PTS, PTS), :], xsem.at[k])

        for copy in panel_copies + [x_copy(k) for k in range(8)] + [acc_copy]:
            copy.start()

        def clear(b, carry):
            out_v[b] = jnp.zeros((WCOL, BLK), F32)
            return carry

        lax.fori_loop(0, BLOCKS + 1, clear, 0)
        for copy in panel_copies:
            copy.wait()
        panel_norms(group, parts, wide, node_norms)

        def arrive(done, upto):
            def wait(k, carry):
                x_copy(k).wait()
                return carry

            lax.fori_loop(done, upto, wait, 0)
            return jnp.maximum(done, upto)

        run_far(group, starts, entries, xs, norm_ref, pan, node_norms, out_v, s0, s1, arrive)
        acc_copy.wait()

        def merge_first(blocks, first=0):
            def merge_one(b, carry):
                out_v[first + b] = out_v[first + b] + acc_v[first + b]
                return carry

            lax.fori_loop(0, blocks, merge_one, 0)

        if last:

            def merge(b, carry):
                c = BLOCKS // 2 + b
                send_v[b] = (out_v[c] + acc_v[c]).astype(BF16)
                return carry

            copies = [
                pltpu.make_async_copy(send_v, send_hbm, osem.at[0]),
                pltpu.make_async_copy(out_v.at[pl.ds(0, BLOCKS // 2)], keep_hbm, osem.at[1]),
            ]
            lax.fori_loop(0, BLOCKS // 2, merge, 0)
            copies[0].start()
            merge_first(BLOCKS // 2)
            copies[1].start()
        else:
            copies = []
            for part in range(4):
                merge_first(BLOCKS // 4, part * BLOCKS // 4)
                rows_out = pl.ds(part * BLOCKS // 4, BLOCKS // 4)
                copies.append(pltpu.make_async_copy(out_v.at[rows_out], out_hbm.at[rows_out], osem.at[part]))
                copies[-1].start()
        for copy in copies:
            copy.wait()

    anys = pl.BlockSpec(memory_space=pltpu.HBM)
    sums = (BLOCKS, WCOL, BLK)
    half = (BLOCKS // 2, WCOL, BLK)
    return pl.pallas_call(
        body,
        grid_spec=pltpu.PrefetchScalarGridSpec(
            num_scalar_prefetch=2,
            grid=(),
            in_specs=[anys, pl.BlockSpec(memory_space=pltpu.VMEM)] + [anys] * (count + 1),
            out_specs=(anys, anys) if last else anys,
            scratch_shapes=[
                pltpu.VMEM((BLOCKS + 1, WCOL, BLK), F32),
                pltpu.VMEM(sums, F32),
                pltpu.VMEM((8 * PTS, E), BF16),
                pltpu.VMEM((panel_nodes(group) * NODE, E), BF16),
                pltpu.VMEM((len(nrows) * 16, E), BF16),
                pltpu.VMEM((len(nrows) * 16, E), F32),
                pltpu.VMEM((panel_nodes(group), RANK), F32),
                pltpu.VMEM((GROUP, BLK, RANK), F32),
                pltpu.VMEM((GROUP, BLK, RANK), F32),
                pltpu.SemaphoreType.DMA((len(rows) + len(nrows),)),
                pltpu.SemaphoreType.DMA((8,)),
                pltpu.SemaphoreType.DMA((4,)),
            ]
            + ([pltpu.VMEM(half, BF16)] if last else []),
        ),
        out_shape=(jax.ShapeDtypeStruct(half, F32), jax.ShapeDtypeStruct(half, BF16))
        if last
        else jax.ShapeDtypeStruct(sums, F32),
        cost_estimate=pl.CostEstimate(
            flops=(5 if last else 10) * 10**9, bytes_accessed=25 * 10**6, transcendentals=6 * 10**6
        ),
    )(starts, entries, x_all, norms, *panels, acc)


def shards(points, weights, near_list, far_list, skel_index, equiv_weights):
    def along_y(d):
        return [(s, ((s // 2 + d) % 4) * 2 + s % 2) for s in range(8)]

    def along_z(d):
        return [(t, ((t // 4 + d) % 4) * 4 + t % 4) for t in range(16)]

    def along_x(d):
        return [(t, (t // 4) * 4 + (t % 4 + d) % 4) for t in range(16)]

    partner = [(s, s ^ 1) for s in range(8)]

    def move(v, axis, pairs):
        return lax.ppermute(v, axis, pairs)

    meta = jnp.stack([lax.axis_index("tgt"), lax.axis_index("src")]).astype(jnp.int32)
    entries, starts = sorted_entries(far_list[:, :, 0].T, lax.axis_index("tgt"), lax.axis_index("src"))
    pack, half_a, half_b = prep(points, weights.T, jnp.swapaxes(equiv_weights, 1, 2), skel_index)

    def first_axis(v, along):
        return [v] + [move(v, "tgt", along(d)) for d in (1, -1, 2)]

    def second_axis(v, along):
        low, high = jnp.concatenate(v[:2], axis=0), jnp.concatenate(v[2:], axis=0)
        up0, down1 = move(low, "tgt", along(1)), move(high, "tgt", along(-1))
        up1, down0 = move(high, "tgt", along(1)), move(low, "tgt", along(-1))
        return [low, high, up0, up1, down0, down1, move(up0, "tgt", along(1)), move(down1, "tgt", along(-1))]

    a4 = first_axis(half_a, along_z)
    b4 = first_axis(half_b, along_x)
    panels = second_axis(a4, along_x) + second_axis(b4, along_z)
    up, down = move(pack, "src", along_y(1)), move(pack, "src", along_y(-1))
    cut = PACK // 2
    mine = [pack, up, down, move(up[:cut], "src", along_y(1)), move(down[cut:], "src", along_y(-1))]
    pieces = mine + [move(v, "src", partner) for v in mine]

    def operands(group):
        kinds = panel_layout(group)
        used = sorted({half * 8 + p for items in kinds for half, p, _, _, _ in items})
        copies = [[(used.index(h * 8 + p), a, r, d) for h, p, a, r, d in items] for items in kinds]
        return [panels[u] for u in used], *copies

    x_all, norms, near_sum, sums0 = near_call(meta, near_list, starts, entries, pieces, *operands(0))
    sums1 = far_call(1, starts, entries, x_all, norms, sums0, *operands(1))
    keep, send = far_call(2, starts, entries, x_all, norms, sums1, *operands(2))

    half = (4, BLK_DEV, WCOL, BLK)
    chip = keep.reshape(half) + move(send, "src", partner).reshape(half).astype(F32)
    out = near_sum + chip[0]
    for i, d in ((1, -1), (2, 1), (3, 2)):
        out = out + move(chip[i].astype(BF16), "src", along_y(d)).astype(F32)
    return out.transpose(0, 2, 1).reshape(PTS, WCOL)


def solution(mesh):
    in_specs = (
        P(("tgt", "src"), None),
        P(("tgt", "src"), None),
        P(("tgt", "src"), None),
        P("tgt", None, "src"),
        P(("tgt", "src"), None),
        P(("tgt", "src"), None, None),
    )
    out_specs = P(("tgt", "src"), None)

    return jax.shard_map(shards, mesh=mesh, in_specs=in_specs, out_specs=out_specs, check_vma=False)
```

```python
import jax
import jax.numpy as jnp
from jax import lax
from jax.experimental import pallas as pl
from jax.experimental.pallas import tpu as pltpu
from jax.sharding import PartitionSpec as P

E = 256
WCOL = 64
BLK = 128
RANK = 256
NEAR = 16
LEVELS = 3
BLK_DEV = 16
NODE_DEV = 7
PTS = BLK_DEV * BLK
WROWS = BLK_DEV * 32 + 32
PACK = PTS + WROWS
NODE = RANK + WCOL
DATA = NODE_DEV * NODE // 2
HALF = DATA + 16
BLOCKS = 8 * BLK_DEV
LOG2E = 1.4426950408889634
DOT_SCALE = 4.0 * LOG2E
NORM_SCALE = 2.0 * LOG2E
DEAD = 1e30
GROUP = 4
SLACK = 3 * GROUP
F32 = jnp.float32
BF16 = jnp.bfloat16
NT = (((1,), (1,)), ((), ()))


def row_norms(x):
    v = x.astype(F32)
    sq = v * v
    half = sq[:, 0:128] + sq[:, 128:256]
    parts = [jnp.sum(half[i : i + 128].T, axis=0, keepdims=True) for i in range(0, x.shape[0], 128)]
    row = parts[0] if len(parts) == 1 else jnp.concatenate(parts, axis=1)
    return row * NORM_SCALE


def column_of(row, copies=2):
    col = jnp.broadcast_to(row, (128, 128)).T
    return jnp.concatenate([col] * copies, axis=1)


def relative(there, here):
    d = (there - here) & 3
    return jnp.where(d == 0, 0, jnp.where(d == 3, 1, d + 1))


def three_parts(v):
    hi = v.astype(BF16).astype(F32)
    mid = (v - hi).astype(BF16).astype(F32)
    return hi, mid, v - hi - mid


def prep_body(pts, wts, ewts, idx, y_out, half_a, half_b, norms):
    def node(r, first, size):
        parts = []
        for c in range(0, RANK, 128):
            want = column_of(idx[r : r + 1, c : c + 128].astype(F32), size // 128)
            iota = lax.broadcasted_iota(jnp.int32, (128, size), 1).astype(F32)
            pick = jnp.where(iota == want - first, 1.0, 0.0).astype(BF16)
            rows = lax.dot_general(
                pick, pts[first : first + size, :], (((1,), (0,)), ((), ())), preferred_element_type=F32
            )
            parts.append(rows.astype(BF16))
        rows = jnp.concatenate(parts, axis=0)
        for c, part in enumerate(three_parts(row_norms(rows))):
            row = (16 if r >= 3 else 0) + c * 4 + (r - 3 if r >= 3 else r)
            norms[row : row + 1, :] = part
        return rows

    norms[...] = jnp.zeros((32, E), F32)
    cut = DATA - 3 * NODE
    for r in range(3):
        half_a[r * NODE : r * NODE + RANK, :] = node(r, r * 512, 512)
        half_a[r * NODE + RANK : (r + 1) * NODE, :] = ewts[r]
    rows = node(3, 3 * 512, 512)
    half_a[3 * NODE : DATA, :] = rows[0:cut]
    half_b[0 : RANK - cut, :] = rows[cut:RANK]
    half_b[RANK - cut : NODE - cut, :] = ewts[3]
    for r, first, size in ((4, 0, 1024), (5, 1024, 1024), (6, 0, 2048)):
        row = r * NODE - DATA
        half_b[row : row + RANK, :] = node(r, first, size)
        half_b[row + RANK : row + NODE, :] = ewts[r]
    half_a[DATA:HALF, :] = norms[0:16, :].astype(BF16)
    half_b[DATA:HALF, :] = norms[16:32, :].astype(BF16)
    y_out[0:PTS, :] = pts[...]
    for b in range(BLK_DEV):
        w = wts[:, b * BLK : (b + 1) * BLK]
        row = PTS + b * 32
        y_out[row : row + 32, 0:BLK] = w[0:32]
        y_out[row : row + 32, BLK:E] = w[32:64]
        for c, part in enumerate(three_parts(row_norms(pts[b * BLK : (b + 1) * BLK, :]))):
            at = b + c // 2 * 16
            norms[at : at + 1, c % 2 * BLK : (c % 2 + 1) * BLK] = part
    norms[16:32, BLK:E] = jnp.zeros((16, BLK), F32)
    y_out[PACK - 32 : PACK, :] = norms[...].astype(BF16)


def prep(points, weights_t, equiv_t, skel_index):
    return pl.pallas_call(
        prep_body,
        out_shape=(
            jax.ShapeDtypeStruct((PACK, E), BF16),
            jax.ShapeDtypeStruct((HALF, E), BF16),
            jax.ShapeDtypeStruct((HALF, E), BF16),
        ),
        scratch_shapes=[pltpu.VMEM((32, E), F32)],
        cost_estimate=pl.CostEstimate(flops=10**9, bytes_accessed=8 * 10**6, transcendentals=0),
        name="prep",
    )(points, weights_t, equiv_t, skel_index)


def run_entries(total, dots, finish, s0, s1, before=None, state=0):
    def pair(j, state):
        first = j * 2 * GROUP
        if before is not None:
            state = before(j, state)
        dots(first + GROUP, s1)
        finish(first, s0)
        dots(first + 2 * GROUP, s0)
        finish(first + GROUP, s1)
        return state

    dots(0, s0)
    return lax.fori_loop(0, (total + 2 * GROUP - 1) // (2 * GROUP), pair, state)


def sorted_entries(far, tgt_index, src_index):
    level = lax.broadcasted_iota(jnp.int32, far.shape, 0)
    b = lax.broadcasted_iota(jnp.int32, far.shape, 1)
    src = b // BLK_DEV
    slot = ((src & 1) ^ (src_index & 1)) * 4 + relative(src // 2, src_index // 2)
    w = jnp.maximum(far, 0)
    owner = w >> (2 - level)
    r = (w & ((4 >> level) - 1)) + jnp.where(level == 0, 0, 2 * level + 2)
    i, j = relative(owner // 4, tgt_index // 4), relative(owner & 3, tgt_index & 3)
    of_i, of_j = jnp.where(i == 3, 2, jnp.minimum(i, 1)), jnp.where(j == 3, 2, jnp.minimum(j, 1))
    cls = jnp.where(r < 3, of_j, jnp.where(r > 3, of_i, jnp.maximum(of_i, of_j)))
    order = [0] * (16 * NODE_DEV)
    for group in range(3):
        for n, (i2, j2, r2) in enumerate(class_nodes(group)):
            order[(i2 * 4 + j2) * NODE_DEV + r2] = n
    place = (i * 4 + j) * NODE_DEV + r
    hit = place[..., None] == jnp.arange(len(order), dtype=jnp.int32)
    node = jnp.sum(jnp.where(hit, jnp.array(order, jnp.int32), 0), axis=-1)
    node = jnp.where(far >= 0, node, level)
    cls = jnp.where(far >= 0, cls, 3).reshape(-1)
    keys = (cls << 14) | ((slot * BLK_DEV + b % BLK_DEV) << 7 | node).reshape(-1)
    rank = jnp.sum((keys[None, :] < keys[:, None]).astype(jnp.int32), axis=1)
    places = jnp.arange(keys.shape[0], dtype=jnp.int32)
    entries = jnp.sum(jnp.where(rank[None, :] == places[:, None], keys[None, :], 0), axis=1)
    starts = jnp.sum((cls[None, :] < jnp.arange(4, dtype=jnp.int32)[:, None]).astype(jnp.int32), axis=1)
    return entries, starts


def class_nodes(group):
    cls = (0, 1, 1, 2)
    grid = [(i, j) for i in range(4) for j in range(4)]
    nodes = [(i, j, r) for i, j in grid if cls[j] == group for r in range(3)]
    nodes += [(i, j, r) for i, j in grid if cls[i] == group for r in range(4, NODE_DEV)]
    return nodes + [(i, j, 3) for i, j in grid if max(cls[i], cls[j]) == group]


def panel_nodes(group):
    return (len(class_nodes(group)) + 3) // 4 * 4


def panel_layout(group):
    cut = DATA - 3 * NODE
    rows, norms = [], []
    for n, (i, j, r) in enumerate(class_nodes(group)):
        if r == 0:
            spans = [(0, 0, 3 * NODE, 0)]
        elif r == 3:
            spans = [(0, DATA - cut, cut, 0), (1, 0, NODE - cut, cut)]
        elif r == 4:
            spans = [(1, NODE - cut, 3 * NODE, 0)]
        else:
            continue
        for half, row, count, place in spans:
            first, second = (i, j) if half == 0 else (j, i)
            rows.append((half, second * 2 + first // 2, (first % 2) * HALF + row, count, n * NODE + place))
        norms.append((half, second * 2 + first // 2, (first % 2) * HALF + DATA, 16, len(norms) * 16))
    return rows, norms


def panel_norms(group, parts, wide, node_norms):
    wide[...] = parts[...].astype(F32)
    k = -1
    for n, (i, j, r) in enumerate(class_nodes(group)):
        if r in (0, 3, 4):
            k += 1
        row = k * 16 + (r if r < 3 else r - 3)
        node_norms[n : n + 1, :] = wide[row : row + 1, :] + wide[row + 4 : row + 5, :] + wide[row + 8 : row + 9, :]


def run_far(group, starts, entries, xs, norm_ref, pan, node_norms, out_v, s0, s1, arrive=None):
    start, end = starts[group], starts[group + 1]

    def entry(e):
        live = start + e < end
        code = entries[jnp.minimum(start + e, BLOCKS * LEVELS - 1)]
        b = jnp.where(live, (code >> 7) & 127, BLOCKS)
        return b, jnp.where(live, code & 127, 0)

    def dots(first, s_ref):
        for u in range(GROUP):
            b, n = entry(first + u)
            b = jnp.minimum(b, BLOCKS - 1)
            x = xs[pl.ds(pl.multiple_of(b * BLK, BLK), BLK), :]
            src = pan[pl.ds(pl.multiple_of(n * NODE, NODE), RANK), :]
            dot = lax.dot_general(x, src, NT, preferred_element_type=F32)
            s_ref[u] = dot * DOT_SCALE - column_of(norm_ref[pl.ds(b, 1), :])

    def finish(first, s_ref):
        for u in range(GROUP):
            b, n = entry(first + u)
            k = jnp.exp2(s_ref[u] - node_norms[pl.ds(n, 1), :]).astype(BF16)
            wt = pan[pl.ds(pl.multiple_of(n * NODE, NODE) + RANK, WCOL), :]
            out_v[b] = out_v[b] + lax.dot_general(wt, k, NT, preferred_element_type=F32)

    if arrive is None:
        run_entries(end - start, dots, finish, s0, s1)
        return

    def needed(e):
        return jnp.minimum(entry(e)[0] // BLK_DEV, 7) + 1

    arrived = arrive(0, needed(GROUP - 1))

    def before(j, arrived):
        return arrive(arrived, needed(j * 2 * GROUP + 3 * GROUP - 1))

    arrived = run_entries(end - start, dots, finish, s0, s1, before, arrived)
    arrive(arrived, 8)


def near_call(meta, near_list, starts, entries, pieces, panels, rows, nrows):
    count = len(panels)

    def body(meta, near, starts, entries, *refs):
        pieces, sources, refs = refs[:10], refs[10 : 10 + count], refs[10 + count :]
        x_out, norm_out, near_out, sums_out, *refs = refs
        xs, ws, pan, parts, wide, node_norms, acc, out_v, s0, s1, targets, slots, sems, wsem, psem, out_sems = refs
        y, core = meta[1] // 2, meta[1] & 1

        def store(k):
            return pltpu.make_async_copy(xs.at[pl.ds(k * PTS, PTS), :], x_out.at[k], out_sems.at[k])

        loads, cut = [], PACK // 2
        for k in range(8):
            p = k // 4 * 5 + k % 4
            spans = [(p, 0, PTS)] if k % 4 < 3 else [(p, 0, cut), (p + 1, cut, PTS - cut)]
            for piece, row, size in spans:
                first = 0 if piece != p + 1 else row - cut
                loads.append(
                    pltpu.make_async_copy(
                        pieces[piece].at[pl.ds(first, size), :], xs.at[pl.ds(k * PTS + row, size), :], sems.at[piece]
                    )
                )
            piece, first = (p, PTS) if k % 4 < 3 else (p + 1, PTS - cut)
            loads.append(
                pltpu.make_async_copy(
                    pieces[piece].at[pl.ds(first, WROWS), :], ws.at[pl.ds(k * WROWS, WROWS), :], wsem.at[k]
                )
            )

        panel_copies = [
            pltpu.make_async_copy(sources[p].at[pl.ds(a, r), :], to.at[pl.ds(d, r), :], psem.at[i])
            for i, (to, p, a, r, d) in enumerate([(pan, *item) for item in rows] + [(parts, *item) for item in nrows])
        ]
        for copy in loads:
            copy.start()

        def scan_near(i, n):
            for p in range(NEAR // 2):
                targets[n] = i
                slots[n] = 2 * p
                n = n + jnp.where(near[i, 2 * p] >= 0, 1, 0)
            acc[i] = jnp.zeros((WCOL, BLK), F32)
            return n

        total = lax.fori_loop(0, BLK_DEV, scan_near, 0)
        for i in range(SLACK):
            targets[total + i] = BLK_DEV
            slots[total + i] = 0
        acc[BLK_DEV] = jnp.zeros((WCOL, BLK), F32)

        def clear(b, carry):
            out_v[b] = jnp.zeros((WCOL, BLK), F32)
            return carry

        lax.fori_loop(0, BLOCKS + 1, clear, 0)
        for k in range(8):
            for copy in (loads[k // 4 * 9 + k % 4 * 2 :])[: 3 if k % 4 == 3 else 2]:
                copy.wait()

            v = ws[pl.ds(k * WROWS + WROWS - 32, 32), :].astype(F32)
            norm_out[pl.ds(k * BLK_DEV, BLK_DEV), :] = v[0:16, 0:BLK] + v[0:16, BLK:E] + v[16:32, 0:BLK]
        for copy in panel_copies:
            copy.start()
        for k in range(8):
            store(k).start()

        def source(i, slot):
            v = near[i, slot]
            j = jnp.maximum(v, 0)
            k = (((j // BLK_DEV) & 1) ^ core) * 4 + relative(j // (2 * BLK_DEV), y)
            return v, k, j % BLK_DEV

        def dots(first, s_ref):
            for u in range(GROUP):
                i = jnp.minimum(targets[first + u], BLK_DEV - 1)
                x = xs[pl.ds(pl.multiple_of(i * BLK, BLK), BLK), :]
                srcs, rows = [], []
                for s in range(2):
                    v, k, b = source(i, slots[first + u] + s)
                    srcs.append(xs[pl.ds(pl.multiple_of(k * PTS + b * BLK, BLK), BLK), :])
                    bias = jnp.where(v >= 0, 0.0, DEAD).astype(F32)
                    rows.append(norm_out[pl.ds(k * BLK_DEV + b, 1), :] + bias)
                dot = lax.dot_general(x, jnp.concatenate(srcs, axis=0), NT, preferred_element_type=F32)
                col = column_of(norm_out[pl.ds(i, 1), :])
                s_ref[u] = dot * DOT_SCALE - col - jnp.concatenate(rows, axis=1)

        def finish(first, s_ref):
            for u in range(GROUP):
                target = targets[first + u]
                i = jnp.minimum(target, BLK_DEV - 1)
                wts = []
                for s in range(2):
                    _, k, b = source(i, slots[first + u] + s)
                    w = ws[pl.ds(pl.multiple_of(k * WROWS + b * 32, 32), 32), :]
                    wts.append(jnp.concatenate([w[:, 0:128], w[:, 128:256]], axis=0))
                k = jnp.exp2(s_ref[u]).astype(BF16)
                acc[target] = acc[target] + lax.dot_general(
                    jnp.concatenate(wts, axis=1), k, NT, preferred_element_type=F32
                )

        run_entries(total, dots, finish, s0, s1)
        near_out[...] = acc[0:BLK_DEV]

        for copy in panel_copies:
            copy.wait()
        panel_norms(0, parts, wide, node_norms)

        run_far(0, starts, entries, xs, norm_out, pan, node_norms, out_v, s0, s1)
        result = pltpu.make_async_copy(out_v.at[pl.ds(0, BLOCKS)], sums_out, out_sems.at[8])
        result.start()
        for k in range(8):
            store(k).wait()
        result.wait()

    anys = pl.BlockSpec(memory_space=pltpu.HBM)
    vm = pl.BlockSpec(memory_space=pltpu.VMEM)
    return pl.pallas_call(
        body,
        grid_spec=pltpu.PrefetchScalarGridSpec(
            num_scalar_prefetch=4,
            grid=(),
            in_specs=[anys] * (10 + count),
            out_specs=[anys, vm, vm, anys],
            scratch_shapes=[
                pltpu.VMEM((8 * PTS, E), BF16),
                pltpu.VMEM((8 * WROWS, E), BF16),
                pltpu.VMEM((panel_nodes(0) * NODE, E), BF16),
                pltpu.VMEM((len(nrows) * 16, E), BF16),
                pltpu.VMEM((len(nrows) * 16, E), F32),
                pltpu.VMEM((panel_nodes(0), RANK), F32),
                pltpu.VMEM((BLK_DEV + 1, WCOL, BLK), F32),
                pltpu.VMEM((BLOCKS + 1, WCOL, BLK), F32),
                pltpu.VMEM((GROUP, BLK, RANK), F32),
                pltpu.VMEM((GROUP, BLK, RANK), F32),
                pltpu.SMEM((BLK_DEV * NEAR // 2 + SLACK,), jnp.int32),
                pltpu.SMEM((BLK_DEV * NEAR // 2 + SLACK,), jnp.int32),
                pltpu.SemaphoreType.DMA((10,)),
                pltpu.SemaphoreType.DMA((8,)),
                pltpu.SemaphoreType.DMA((len(rows) + len(nrows),)),
                pltpu.SemaphoreType.DMA((9,)),
            ],
        ),
        out_shape=[
            jax.ShapeDtypeStruct((8, PTS, E), BF16),
            jax.ShapeDtypeStruct((BLOCKS, BLK), F32),
            jax.ShapeDtypeStruct((BLK_DEV, WCOL, BLK), F32),
            jax.ShapeDtypeStruct((BLOCKS, WCOL, BLK), F32),
        ],
        cost_estimate=pl.CostEstimate(flops=9 * 10**9, bytes_accessed=30 * 10**6, transcendentals=6 * 10**6),
        name="near",
    )(meta, near_list, starts, entries, *pieces, *panels)


def far_call(group, starts, entries, x_all, norms, acc, panels, rows, nrows):
    count = len(panels)
    last = group == 2

    def body(starts, entries, x_hbm, norm_ref, *refs):
        sources, acc_hbm, refs = refs[:count], refs[count], refs[count + 1 :]
        if last:
            keep_hbm, send_hbm, *refs, send_v = refs
        else:
            out_hbm, *refs = refs
        out_v, acc_v, xs, pan, parts, wide, node_norms, s0, s1, psem, xsem, osem = refs
        panel_copies = [
            pltpu.make_async_copy(sources[p].at[pl.ds(a, r), :], to.at[pl.ds(d, r), :], psem.at[i])
            for i, (to, p, a, r, d) in enumerate([(pan, *item) for item in rows] + [(parts, *item) for item in nrows])
        ]
        acc_copy = pltpu.make_async_copy(acc_hbm, acc_v, osem.at[0])

        def x_copy(k):
            return pltpu.make_async_copy(x_hbm.at[k], xs.at[pl.ds(k * PTS, PTS), :], xsem.at[k])

        for copy in panel_copies + [x_copy(0)]:
            copy.start()

        def clear(b, carry):
            out_v[b] = jnp.zeros((WCOL, BLK), F32)
            return carry

        lax.fori_loop(0, BLOCKS + 1, clear, 0)
        for copy in panel_copies:
            copy.wait()
        for copy in [x_copy(k) for k in range(1, 8)] + [acc_copy]:
            copy.start()
        panel_norms(group, parts, wide, node_norms)

        def arrive(done, upto):
            def wait(k, carry):
                x_copy(k).wait()
                return carry

            lax.fori_loop(done, upto, wait, 0)
            return jnp.maximum(done, upto)

        run_far(group, starts, entries, xs, norm_ref, pan, node_norms, out_v, s0, s1, arrive)
        acc_copy.wait()

        def merge_first(blocks, first=0):
            def merge_one(b, carry):
                out_v[first + b] = out_v[first + b] + acc_v[first + b]
                return carry

            lax.fori_loop(0, blocks, merge_one, 0)

        if last:

            def merge(b, carry):
                c = BLOCKS // 2 + b
                send_v[b] = (out_v[c] + acc_v[c]).astype(BF16)
                return carry

            copies = [
                pltpu.make_async_copy(send_v, send_hbm, osem.at[0]),
                pltpu.make_async_copy(out_v.at[pl.ds(0, BLOCKS // 2)], keep_hbm, osem.at[1]),
            ]
            lax.fori_loop(0, BLOCKS // 2, merge, 0)
            copies[0].start()
            merge_first(BLOCKS // 2)
            copies[1].start()
        else:
            copies = []
            for part in range(4):
                merge_first(BLOCKS // 4, part * BLOCKS // 4)
                rows_out = pl.ds(part * BLOCKS // 4, BLOCKS // 4)
                copies.append(pltpu.make_async_copy(out_v.at[rows_out], out_hbm.at[rows_out], osem.at[part]))
                copies[-1].start()
        for copy in copies:
            copy.wait()

    anys = pl.BlockSpec(memory_space=pltpu.HBM)
    sums = (BLOCKS, WCOL, BLK)
    half = (BLOCKS // 2, WCOL, BLK)
    return pl.pallas_call(
        body,
        grid_spec=pltpu.PrefetchScalarGridSpec(
            num_scalar_prefetch=2,
            grid=(),
            in_specs=[anys, pl.BlockSpec(memory_space=pltpu.VMEM)] + [anys] * (count + 1),
            out_specs=(anys, anys) if last else anys,
            scratch_shapes=[
                pltpu.VMEM((BLOCKS + 1, WCOL, BLK), F32),
                pltpu.VMEM(sums, F32),
                pltpu.VMEM((8 * PTS, E), BF16),
                pltpu.VMEM((panel_nodes(group) * NODE, E), BF16),
                pltpu.VMEM((len(nrows) * 16, E), BF16),
                pltpu.VMEM((len(nrows) * 16, E), F32),
                pltpu.VMEM((panel_nodes(group), RANK), F32),
                pltpu.VMEM((GROUP, BLK, RANK), F32),
                pltpu.VMEM((GROUP, BLK, RANK), F32),
                pltpu.SemaphoreType.DMA((len(rows) + len(nrows),)),
                pltpu.SemaphoreType.DMA((8,)),
                pltpu.SemaphoreType.DMA((4,)),
            ]
            + ([pltpu.VMEM(half, BF16)] if last else []),
        ),
        out_shape=(jax.ShapeDtypeStruct(half, F32), jax.ShapeDtypeStruct(half, BF16))
        if last
        else jax.ShapeDtypeStruct(sums, F32),
        cost_estimate=pl.CostEstimate(
            flops=(5 if last else 10) * 10**9, bytes_accessed=25 * 10**6, transcendentals=6 * 10**6
        ),
    )(starts, entries, x_all, norms, *panels, acc)


def shards(points, weights, near_list, far_list, skel_index, equiv_weights):
    def along_y(d):
        return [(s, ((s // 2 + d) % 4) * 2 + s % 2) for s in range(8)]

    def along_z(d):
        return [(t, ((t // 4 + d) % 4) * 4 + t % 4) for t in range(16)]

    def along_x(d):
        return [(t, (t // 4) * 4 + (t % 4 + d) % 4) for t in range(16)]

    partner = [(s, s ^ 1) for s in range(8)]

    def move(v, axis, pairs):
        return lax.ppermute(v, axis, pairs)

    meta = jnp.stack([lax.axis_index("tgt"), lax.axis_index("src")]).astype(jnp.int32)
    entries, starts = sorted_entries(far_list[:, :, 0].T, lax.axis_index("tgt"), lax.axis_index("src"))
    pack, half_a, half_b = prep(points, weights.T, jnp.swapaxes(equiv_weights, 1, 2), skel_index)

    def first_axis(v, along):
        return [v] + [move(v, "tgt", along(d)) for d in (1, -1, 2)]

    def second_axis(v, along):
        low, high = jnp.concatenate(v[:2], axis=0), jnp.concatenate(v[2:], axis=0)
        up0, down1 = move(low, "tgt", along(1)), move(high, "tgt", along(-1))
        up1, down0 = move(high, "tgt", along(1)), move(low, "tgt", along(-1))
        return [low, high, up0, up1, down0, down1, move(up0, "tgt", along(1)), move(down1, "tgt", along(-1))]

    a4 = first_axis(half_a, along_z)
    b4 = first_axis(half_b, along_x)
    panels = second_axis(a4, along_x) + second_axis(b4, along_z)
    up, down = move(pack, "src", along_y(1)), move(pack, "src", along_y(-1))
    cut = PACK // 2
    mine = [pack, up, down, move(up[:cut], "src", along_y(1)), move(down[cut:], "src", along_y(-1))]
    pieces = mine + [move(v, "src", partner) for v in mine]

    def operands(group):
        kinds = panel_layout(group)
        used = sorted({half * 8 + p for items in kinds for half, p, _, _, _ in items})
        copies = [[(used.index(h * 8 + p), a, r, d) for h, p, a, r, d in items] for items in kinds]
        return [panels[u] for u in used], *copies

    x_all, norms, near_sum, sums0 = near_call(meta, near_list, starts, entries, pieces, *operands(0))
    sums1 = far_call(1, starts, entries, x_all, norms, sums0, *operands(1))
    keep, send = far_call(2, starts, entries, x_all, norms, sums1, *operands(2))

    half = (4, BLK_DEV, WCOL, BLK)
    chip = keep.reshape(half) + move(send, "src", partner).reshape(half).astype(F32)
    out = near_sum + chip[0]
    for i, d in ((1, -1), (2, 1), (3, 2)):
        out = out + move(chip[i].astype(BF16), "src", along_y(d)).astype(F32)
    return out.transpose(0, 2, 1).reshape(PTS, WCOL)


def solution(mesh):
    in_specs = (
        P(("tgt", "src"), None),
        P(("tgt", "src"), None),
        P(("tgt", "src"), None),
        P("tgt", None, "src"),
        P(("tgt", "src"), None),
        P(("tgt", "src"), None, None),
    )
    out_specs = P(("tgt", "src"), None)

    return jax.shard_map(shards, mesh=mesh, in_specs=in_specs, out_specs=out_specs, check_vma=False)
```
